128 devices in a mesh: row: 8 (over z, y_lo), col: 16 (over y_hi, x, core).
Axes of the slice: x: 4, y: 4 (y_hi: 2, y_lo: 2; y = y_hi * 2 + y_lo), z: 4, core: 2. Of those that a mesh axis runs over, the one named last changes fastest.
Arguments:
- orbitals: bfloat16 [32, 64, 512], P('row', 'col'), may hold values from -6 to 6
- screened: bfloat16 [16384, 512], P(('row', 'col')), may hold values from -2.1579186e-05 to 2.1579186e-05
- kpoints: int32 [32], replicated, may hold values from 0 to 31, each once
- vectors: bfloat16 [64, 32768], P(None, ('row', 'col')), may hold values from -6 to 6
- energies: float32 [32, 64], replicated, may hold values from -1 to 1
Outputs:
- filtered: float32 [64, 32768], P(None, ('row', 'col'))
The draws below stay inside these ranges and needn't reach their ends.
All inputs are finite; a program needn't handle non-finite values.
Results may differ from the reference program's by a relative error of at most 0.0034.
Values may be sent and summed in bfloat16 or wider, within the bound.
A program may use at most 128 MiB of HBM per device.

```python
import jax
import jax.numpy as jnp
from jax import lax

NV = 32
NC = 32
NG = 512
NX = 64
NK = 32
NB = 64


def draw_screened(key, part):
    spread_value = 0.5 / (NG * (NK * NV * NC) ** 0.5)
    values = jnp.clip(jax.random.normal(key, (NK * NG, NG), jnp.float32), -4.0, 4.0)
    return (values * spread_value).astype(jnp.bfloat16)


def steps_of(stream_key, dims, shards, low, largest):
    factor_of = 1.0
    for axis_at, blocks in shards:
        heights = jax.random.uniform(jax.random.fold_in(jax.random.fold_in(stream_key, 6), axis_at), (blocks,), jnp.float32, low / len(shards), largest / len(shards))
        factor_of = factor_of * jnp.repeat(jnp.exp(heights), dims[axis_at] // blocks).reshape((-1,) + (1,) * (len(dims) - 1 - axis_at))
    return factor_of


def bell_draw(rng, extent, width, limit, shards=(), kind=jnp.bfloat16):
    result = width * jax.random.normal(rng, extent, jnp.float32)
    if shards:
        result = result * steps_of(rng, extent, shards, -0.22, 0.18)
    return jnp.clip(result, -limit, limit).astype(kind)


def setup_inputs(seed: int = 0) -> dict:
    keys = jax.random.split(jax.random.key(seed), 6)
    return {
        "orbitals": bell_draw(keys[0], (NK, NB, NG), 1.0, 6.0, ((0, 8), (1, 16))),
        "screened": draw_screened(jax.random.fold_in(keys[5], 71), 0),
        "kpoints": jax.random.permutation(keys[2], NK).astype(jnp.int32),
        "vectors": bell_draw(keys[3], (NX, NK * NV * NC), 1.0, 6.0, ((1, 128),)),
        "energies": jnp.clip(jax.random.uniform(keys[4], (NK, NB), jnp.float32, -1.0, 1.0), -1.0, 1.0),
    }


SPREAD = 4.0


def pair_tile(orbit_left, orbit_right, screen_block):
    valence = orbit_left[:NV].astype(jnp.float32)[:, None, :] * orbit_right[:NV].astype(jnp.float32)[None, :, :]
    conduct = orbit_left[NV:].astype(jnp.float32)[:, None, :] * orbit_right[NV:].astype(jnp.float32)[None, :, :]
    valence = valence.reshape(NV * NV, NG).astype(jnp.bfloat16)
    conduct = conduct.reshape(NC * NC, NG).astype(jnp.bfloat16)
    amplitude = jnp.dot(valence, screen_block, preferred_element_type=jnp.float32).astype(jnp.bfloat16)
    inner_tile = jnp.dot(amplitude, conduct.T, preferred_element_type=jnp.float32)
    inner_tile = inner_tile.reshape(NV, NV, NC, NC).transpose(0, 2, 1, 3)
    return inner_tile.reshape(NV * NC, NV * NC).astype(jnp.bfloat16)


def apply_kernel(orbitals, screened, kpoints, rounded):
    shaped = rounded.reshape(NX, NK, NV * NC)

    def row_apply(left_index):
        def column_step(running, right_index):
            momentum = ((kpoints[left_index] - kpoints[right_index] + NK) % NK).astype(jnp.int32)
            screen_block = lax.dynamic_slice_in_dim(screened, momentum * NG, NG, 0)
            tile_value = pair_tile(orbitals[left_index], orbitals[right_index], screen_block)
            column = lax.dynamic_index_in_dim(shaped, right_index, 1, keepdims=False)
            return running + jnp.dot(column, tile_value.T, preferred_element_type=jnp.float32), None

        running, unused = lax.scan(column_step, jnp.zeros((NX, NV * NC), jnp.float32), jnp.arange(NK, dtype=jnp.int32))
        return running

    stacked = lax.map(row_apply, jnp.arange(NK, dtype=jnp.int32))
    return stacked.transpose(1, 0, 2).reshape(NX, NK * NV * NC)


def reference(orbitals, screened, kpoints, vectors, energies):
    gap_full = (energies[:, NV:][:, None, :] - energies[:, :NV][:, :, None]).reshape(NK * NV * NC)

    def hamilton(current, rounded):
        return (gap_full * current + apply_kernel(orbitals, screened, kpoints, rounded)) / SPREAD

    state_first = vectors.astype(jnp.float32)
    second = hamilton(state_first, vectors)
    state_third = 2.0 * hamilton(second, second.astype(jnp.bfloat16)) - state_first
    return 2.0 * hamilton(state_third, state_third.astype(jnp.bfloat16)) - second
```

```python
import jax
import jax.numpy as jnp
from jax import lax
from jax.experimental import pallas as pl
from jax.experimental.pallas import tpu as pltpu
from jax.sharding import PartitionSpec as P

NV = 32
NC = 32
NG = 512
NX = 64
NK = 32
PAIRS = NV * NC
ROWS = 8
COLS = 16
SPREAD = 4.0


def column_value(col, t):
    return col // 2 + 8 * lax.rem(col, 2) + 16 * t


def remote(src, dst, send_sem, recv_sem, row, col):
    return pltpu.make_async_remote_copy(
        src_ref=src,
        dst_ref=dst,
        send_sem=send_sem,
        recv_sem=recv_sem,
        device_id=(row, col),
        device_id_type=pl.DeviceIdType.MESH,
    )


def gather_kernel(
    place,
    orb_ref,
    screen_ref,
    vec_ref,
    orb_out,
    screen_out,
    vec_out,
    own_out,
    orb_all,
    staged,
    landed,
    wide,
    vec_all,
    vec_staged,
    s1,
    r1,
    s2,
    r2,
    sw,
    rw,
    lw,
    sv,
    rv,
    sx,
    rx,
):
    a = lax.axis_index("row")
    b = lax.axis_index("col")
    quarter = lax.rem(b, 4)
    group = b // 4

    def first_copy(d):
        return remote(
            orb_ref,
            orb_all.at[pl.ds(4 * a, 4)],
            s1.at[d],
            r1.at[d],
            lax.rem(a + d + 1, ROWS),
            b,
        )

    @pl.loop(0, ROWS - 1)
    def _(d):
        first_copy(d).start()

    orb_all[pl.ds(4 * a, 4)] = orb_ref[...]

    residue = lax.rem(4 * lax.rem(a, 2) + group, 8)
    piece = (a // 2) * 4 + quarter

    def screen_target(i):
        row = lax.rem(a + i // 2, ROWS)
        col = 2 * lax.rem(row - residue + 8, 8) + lax.rem(i, 2)
        return row, col

    def screen_copy(i):
        row, col = screen_target(i)
        return remote(screen_ref, screen_out.at[piece], sw.at[i], rw.at[piece], row, col)

    def screen_local():
        return pltpu.make_async_copy(screen_ref, screen_out.at[piece], lw)

    def is_self(i):
        row, col = screen_target(i)
        return jnp.logical_and(row == a, col == b)

    @pl.loop(0, ROWS - 1)
    def _(d):
        first_copy(d).wait()

    @pl.loop(0, COLS)
    def _(dest):
        for m in range(4):
            staged[dest, m] = orb_all[place[a + 8 * m]]
        for t in range(2):
            staged[dest, 4 + t] = orb_all[place[column_value(dest, t)]]

    def second_copy(d):
        col = lax.rem(b + d + 1, COLS)
        return remote(staged.at[col], landed.at[b], s2.at[d], r2.at[d], a, col)

    @pl.loop(0, COLS - 1)
    def _(d):
        second_copy(d).start()

    @pl.loop(0, 16)
    def _(i):
        @pl.when(is_self(i))
        def _():
            screen_local().start()

        @pl.when(jnp.logical_not(is_self(i)))
        def _():
            screen_copy(i).start()

    landed[b] = staged[b]

    mine = a * 4 + group

    def vector_copy(d):
        other = lax.rem(mine + d + 1, NK)
        return remote(
            vec_ref,
            vec_all.at[mine],
            sv.at[d],
            rv.at[d],
            other // 4,
            4 * lax.rem(other, 4) + quarter,
        )

    @pl.loop(0, NK - 1)
    def _(d):
        vector_copy(d).start()

    vec_all[mine] = vec_ref[...]

    @pl.loop(0, COLS - 1)
    def _(d):
        second_copy(d).wait()

    @pl.loop(0, 6)
    def _(slot):
        for source in range(COLS):
            wide[source * 16 : source * 16 + 16] = landed[source, slot].astype(jnp.float32)
        for part in range(4):
            orb_out[slot, :, part * 128 : part * 128 + 128] = wide[pl.ds(part, 64, stride=4), :]

    @pl.loop(0, NK - 1)
    def _(d):
        vector_copy(d).wait()

    own_out[...] = vec_all[place[a + 8 * group]]

    def spread_copy(d):
        col = 4 * group + lax.rem(quarter + d + 1, 4)
        return remote(vec_staged.at[d], vec_out.at[quarter], sx.at[d], rx.at[d], a, col)

    for d in range(3):
        col = 4 * group + lax.rem(quarter + d + 1, 4)
        for t in range(2):
            vec_staged[d, t] = vec_all[place[column_value(col, t)]]
        spread_copy(d).start()
    for t in range(2):
        vec_out[quarter, t] = vec_all[place[column_value(b, t)]]

    needed = lax.rem(a - b // 2 + 8, 8)
    @pl.loop(0, 16)
    def _(p):
        own_piece = jnp.logical_and(needed == residue, p == piece)

        @pl.when(own_piece)
        def _():
            screen_local().wait()

        @pl.when(jnp.logical_not(own_piece))
        def _():
            remote(screen_ref, screen_out.at[p], sw.at[p], rw.at[p], a, lax.rem(b + 1, COLS)).wait_recv()

    @pl.loop(0, 16)
    def _(i):
        @pl.when(jnp.logical_not(is_self(i)))
        def _():
            screen_copy(i).wait_send()

    for d in range(3):
        spread_copy(d).wait()


def gathered(place, orbitals, screened, vectors):
    dma = pltpu.SemaphoreType.DMA
    vmem = pl.BlockSpec(memory_space=pltpu.VMEM)
    return pl.pallas_call(
        gather_kernel,
        out_shape=(
            jax.ShapeDtypeStruct((6, 64, NG), jnp.float32),
            jax.ShapeDtypeStruct((16, 128, NG), jnp.bfloat16),
            jax.ShapeDtypeStruct((4, 2, NX, 256), jnp.bfloat16),
            jax.ShapeDtypeStruct((NX, 256), jnp.bfloat16),
        ),
        in_specs=[pl.BlockSpec(memory_space=pltpu.SMEM), vmem, vmem, vmem],
        out_specs=(vmem, vmem, vmem, vmem),
        scratch_shapes=[
            pltpu.VMEM((NK, 16, 128), jnp.bfloat16),
            pltpu.VMEM((COLS, 6, 16, 128), jnp.bfloat16),
            pltpu.VMEM((COLS, 6, 16, 128), jnp.bfloat16),
            pltpu.VMEM((256, 128), jnp.float32),
            pltpu.VMEM((NK, NX, 256), jnp.bfloat16),
            pltpu.VMEM((3, 2, NX, 256), jnp.bfloat16),
            dma((7,)),
            dma((7,)),
            dma((15,)),
            dma((15,)),
            dma((16,)),
            dma((16,)),
            dma,
            dma((31,)),
            dma((31,)),
            dma((3,)),
            dma((3,)),
        ],
        compiler_params=pltpu.CompilerParams(has_side_effects=True, vmem_limit_bytes=48 << 20),
        name="gather",
    )(place, orbitals, screened, vectors)


def tile_kernel(slots, orb_left, orb_right, screen_ref, out_ref, valence, conduct, amplitude, product):
    pair = pl.program_id(0)
    slot = slots[pair]
    for v in range(NV):
        valence[v * 32 : v * 32 + 32] = (orb_left[0, v : v + 1] * orb_right[0, :NV]).astype(jnp.bfloat16)
        conduct[v * 32 : v * 32 + 32] = (orb_right[0, NV + v : NV + v + 1] * orb_left[0, NV:]).astype(
            jnp.bfloat16
        )
    amplitude[...] = jnp.dot(
        valence[...], screen_ref[slot], preferred_element_type=jnp.float32
    ).astype(jnp.bfloat16)
    lane = lax.broadcasted_iota(jnp.int32, (32, 128), 1)
    low = lane < 64
    even = lax.rem(lane // 32, 2) == 0
    for block in range(4):
        product[...] = lax.dot_general(
            amplitude[...],
            conduct[block * 256 : block * 256 + 256],
            (((1,), (1,)), ((), ())),
            preferred_element_type=jnp.float32,
        )
        for group in range(8):
            for half in range(2):
                s = [
                    product[group * 128 + i * 32 : group * 128 + i * 32 + 32, half * 128 : half * 128 + 128]
                    for i in range(4)
                ]
                u0 = jnp.where(low, s[0], pltpu.roll(s[2], 64, 1))
                u2 = jnp.where(low, pltpu.roll(s[0], 64, 1), s[2])
                u1 = jnp.where(low, s[1], pltpu.roll(s[3], 64, 1))
                u3 = jnp.where(low, pltpu.roll(s[1], 64, 1), s[3])
                t = [
                    jnp.where(even, u0, pltpu.roll(u1, 32, 1)),
                    jnp.where(even, pltpu.roll(u0, 96, 1), u1),
                    jnp.where(even, u2, pltpu.roll(u3, 32, 1)),
                    jnp.where(even, pltpu.roll(u2, 96, 1), u3),
                ]
                first = block * 256 + half * 128
                lanes = (group % 2) * 128
                for i in range(4):
                    out_ref[group // 2, first + i * 32 : first + i * 32 + 32, lanes : lanes + 128] = t[i].astype(
                        jnp.bfloat16
                    )


def tiles(slots, orbitals, screened):
    return pl.pallas_call(
        tile_kernel,
        out_shape=jax.ShapeDtypeStruct((16, 2 * PAIRS, 256), jnp.bfloat16),
        grid_spec=pltpu.PrefetchScalarGridSpec(
            num_scalar_prefetch=1,
            grid=(8,),
            in_specs=[
                pl.BlockSpec((1, 64, NG), lambda i, s: (i // 2, 0, 0)),
                pl.BlockSpec((1, 64, NG), lambda i, s: (4 + i % 2, 0, 0)),
                pl.BlockSpec((4, NG, NG), lambda i, s: (0, 0, 0)),
            ],
            out_specs=pl.BlockSpec((4, PAIRS, 256), lambda i, s: (i // 2, i % 2, 0)),
            scratch_shapes=[
                pltpu.VMEM((PAIRS, NG), jnp.bfloat16),
                pltpu.VMEM((PAIRS, NG), jnp.bfloat16),
                pltpu.VMEM((PAIRS, NG), jnp.bfloat16),
                pltpu.VMEM((PAIRS, 256), jnp.float32),
            ],
        ),
        compiler_params=pltpu.CompilerParams(vmem_limit_bytes=48 << 20),
        name="tiles",
    )(slots, orbitals, orbitals, screened.reshape(4, NG, NG))


def filter_kernel(
    value,
    kern_ref,
    vec_ref,
    own_ref,
    gap_ref,
    out_ref,
    swap,
    column,
    ordered,
    sent,
    got,
    rounded,
    state,
    final_row,
    final_out,
    final_in,
    sp,
    rp,
    sg,
    rg,
    lg,
    sa,
    ra,
    sb,
    rb,
):
    a = lax.axis_index("row")
    b = lax.axis_index("col")
    quarter = lax.rem(b, 4)
    group = b // 4

    @pl.loop(0, 8)
    def _(i):
        row = lax.broadcasted_iota(jnp.int32, (128, PAIRS), 0) + i * 128
        col = lax.broadcasted_iota(jnp.int32, (128, PAIRS), 1)
        source = lax.rem(col, 32) * 32 + col // 32
        swap[pl.ds(pl.multiple_of(i * 128, 128), 128)] = jnp.where(row == source, 1.0, 0.0).astype(jnp.bfloat16)

    owner_col = 2 * a + lax.rem(group, 2)
    owner_slot = group // 2
    mine = own_ref[...].astype(jnp.float32)
    gap = gap_ref[...]

    def partial_copy(step, d):
        col = lax.rem(b + d + 1, COLS)
        return remote(sent.at[step, d], got.at[step, b], sp.at[step, d], rp.at[step, d], a, col)

    def spread_target(i):
        row = lax.rem(a + i, ROWS)
        return row, jnp.logical_and(row == a, owner_col == b)

    def spread_copy(step, i):
        row, _ = spread_target(i)
        return remote(
            rounded.at[step],
            column.at[step, owner_slot * 4 + quarter],
            sg.at[step, i],
            rg.at[step, owner_slot * 4 + quarter],
            row,
            owner_col,
        )

    for step in range(3):
        for t in range(2):
            block = jnp.zeros((NX, PAIRS), jnp.float32)
            for j in range(4):
                part = vec_ref[j, t] if step == 0 else column[step - 1, t * 4 + j]
                block += jnp.dot(
                    part, swap[j * 256 : j * 256 + 256], preferred_element_type=jnp.float32
                )
            ordered[:, t * PAIRS : t * PAIRS + PAIRS] = block.astype(jnp.bfloat16)

        @pl.loop(0, COLS)
        def _(d):
            col = lax.rem(b + d + 1, COLS)
            part = jnp.dot(ordered[...], kern_ref[col], preferred_element_type=jnp.float32)
            sent[step, d] = part.astype(jnp.bfloat16)

            @pl.when(d < COLS - 1)
            def _():
                partial_copy(step, d).start()

        @pl.loop(0, COLS - 1)
        def _(d):
            partial_copy(step, d).wait()

        got[step, b] = sent[step, COLS - 1]
        total = jnp.zeros((NX, 256), jnp.float32)
        for source in range(COLS):
            total += got[step, source].astype(jnp.float32)
        if step == 0:
            second = (gap * mine + total) / SPREAD
            state[0] = second
            new = second
        elif step == 1:
            third = 2.0 * ((gap * state[0] + total) / SPREAD) - mine
            state[1] = third
            new = third
        else:
            new = 2.0 * ((gap * state[1] + total) / SPREAD) - state[0]
        if step < 2:
            rounded[step] = new.astype(jnp.bfloat16)

            @pl.loop(0, ROWS)
            def _(i):
                _, here = spread_target(i)

                @pl.when(here)
                def _():
                    pltpu.make_async_copy(
                        rounded.at[step], column.at[step, owner_slot * 4 + quarter], lg.at[step]
                    ).start()

                @pl.when(jnp.logical_not(here))
                def _():
                    spread_copy(step, i).start()

            @pl.loop(0, 8)
            def _(p):
                owner = b // 2
                owner_group = lax.rem(b, 2) + 2 * (p // 4)
                here = jnp.logical_and(owner == a, 4 * owner_group + lax.rem(p, 4) == b)

                @pl.when(here)
                def _():
                    pltpu.make_async_copy(rounded.at[step], column.at[step, p], lg.at[step]).wait()

                @pl.when(jnp.logical_not(here))
                def _():
                    remote(
                        rounded.at[step],
                        column.at[step, p],
                        sg.at[step, p],
                        rg.at[step, p],
                        lax.rem(a + 1, ROWS),
                        b,
                    ).wait_recv()
        else:
            final_row[group] = new

    def row_copy(d):
        col = lax.rem(b + 4 * (d + 1), COLS)
        return remote(final_row.at[group], final_row.at[group], sa.at[d], ra.at[d], a, col)

    for d in range(3):
        row_copy(d).start()
    for step in range(2):

        @pl.loop(0, ROWS)
        def _(i):
            _, here = spread_target(i)

            @pl.when(jnp.logical_not(here))
            def _():
                spread_copy(step, i).wait_send()

    for d in range(3):
        row_copy(d).wait()

    def last_copy(d):
        return remote(
            final_out.at[d], final_in.at[a], sb.at[d], rb.at[d], lax.rem(a + d + 1, ROWS), b
        )

    for d in range(7):
        final_out[d] = final_row[value[4 * lax.rem(a + d + 1, ROWS) + group] // 8]
        last_copy(d).start()
    final_in[a] = final_row[value[4 * a + group] // 8]
    for d in range(7):
        last_copy(d).wait()
    out_ref[...] = final_in[lax.rem(value[4 * a + group], 8)]


def filtered(value, kernel_tiles, vectors, own, gap):
    dma = pltpu.SemaphoreType.DMA
    vmem = pl.BlockSpec(memory_space=pltpu.VMEM)
    return pl.pallas_call(
        filter_kernel,
        out_shape=jax.ShapeDtypeStruct((NX, 256), jnp.float32),
        in_specs=[pl.BlockSpec(memory_space=pltpu.SMEM), vmem, vmem, vmem, vmem],
        out_specs=vmem,
        scratch_shapes=[
            pltpu.VMEM((PAIRS, PAIRS), jnp.bfloat16),
            pltpu.VMEM((2, 8, NX, 256), jnp.bfloat16),
            pltpu.VMEM((NX, 2 * PAIRS), jnp.bfloat16),
            pltpu.VMEM((3, COLS, NX, 256), jnp.bfloat16),
            pltpu.VMEM((3, COLS, NX, 256), jnp.bfloat16),
            pltpu.VMEM((2, NX, 256), jnp.bfloat16),
            pltpu.VMEM((2, NX, 256), jnp.float32),
            pltpu.VMEM((4, NX, 256), jnp.float32),
            pltpu.VMEM((7, NX, 256), jnp.float32),
            pltpu.VMEM((8, NX, 256), jnp.float32),
            dma((3, 15)),
            dma((3, 15)),
            dma((2, 8)),
            dma((2, 8)),
            dma((2,)),
            dma((3,)),
            dma((3,)),
            dma((7,)),
            dma((7,)),
        ],
        compiler_params=pltpu.CompilerParams(has_side_effects=True, vmem_limit_bytes=56 << 20),
        name="filter",
    )(value, kernel_tiles, vectors, own, gap)


def per_device(orbitals, screened, kpoints, vectors, energies):
    a = lax.axis_index("row")
    b = lax.axis_index("col")
    points = jnp.arange(NK, dtype=jnp.int32)
    place = jnp.sum(jnp.where(kpoints[None, :] == points[:, None], points[None, :], 0), axis=1, dtype=jnp.int32)
    orb, screen, column, own = gathered(place, orbitals.reshape(4, 16, 128), screened, vectors)

    pair = jnp.arange(8, dtype=jnp.int32)
    carry = jnp.where(a >= b // 2, 0, -1)
    slots = (carry + pair // 2 - b % 2 - 2 * (pair % 2) + 8) % 4
    kernel_tiles = tiles(slots, orb, screen)

    level = lax.dynamic_index_in_dim(energies, place[a + 8 * (b // 4)], 0, keepdims=False)
    valence = lax.dynamic_slice_in_dim(level, (b % 4) * 8, 8, 0)
    gap = (level[None, NV:] - valence[:, None]).reshape(1, 256)
    return filtered(kpoints, kernel_tiles, column, own, gap)


def solution(mesh):
    placed = (P("row", "col", None), P(("row", "col"), None), P(), P(None, ("row", "col")), P())
    return jax.shard_map(
        per_device, mesh=mesh, in_specs=placed, out_specs=P(None, ("row", "col")), check_vma=False
    )
```

```python
import jax
import jax.numpy as jnp
from jax import lax
from jax.experimental import pallas as pl
from jax.experimental.pallas import tpu as pltpu
from jax.sharding import PartitionSpec as P

NV = 32
NC = 32
NG = 512
NX = 64
NK = 32
PAIRS = NV * NC
ROWS = 8
COLS = 16
SPREAD = 4.0
QUART = PAIRS // 4


def column_value(col, t):
    return col // 2 + 8 * lax.rem(col, 2) + 16 * t


def remote(src, dst, send_sem, recv_sem, row, col):
    return pltpu.make_async_remote_copy(
        src_ref=src,
        dst_ref=dst,
        send_sem=send_sem,
        recv_sem=recv_sem,
        device_id=(row, col),
        device_id_type=pl.DeviceIdType.MESH,
    )


def kernel(
    value,
    energy,
    orb_ref,
    screen_ref,
    vec_ref,
    out_ref,
    place,
    wide,
    orb_mine,
    orb_all,
    staged,
    landed,
    orb,
    screen,
    valence,
    conduct,
    amplitude,
    product,
    tiles,
    swap,
    vec_row,
    vec_sent,
    vec_got,
    own,
    gap,
    passed,
    column,
    ordered,
    sent,
    got,
    rounded,
    state,
    final_row,
    final_sent,
    final_got,
    s1,
    r1,
    s2,
    r2,
    sw,
    rw,
    lw,
    sf,
    sva,
    rva,
    lva,
    svb,
    rvb,
    st,
    rt,
    lt,
    sg,
    rg,
    lg,
    sp,
    rp,
    sa,
    ra,
    sb,
    rb,
):
    a = lax.axis_index("row")
    b = lax.axis_index("col")
    quarter = lax.rem(b, 4)
    group = b // 4
    chip = b // 2
    core = lax.rem(b, 2)
    level = a // 2

    for k in range(4):
        for part in range(4):
            wide[pl.ds(k * 16 + part, 4, stride=4), :] = orb_ref[k, :, part * 128 : part * 128 + 128].astype(
                jnp.float32
            )
    for k in range(4):
        orb_mine[k] = wide[k * 16 : k * 16 + 16].astype(jnp.bfloat16)

    def first_copy(d):
        return remote(
            orb_mine, orb_all.at[pl.ds(4 * a, 4)], s1.at[d], r1.at[d], lax.rem(a + d + 1, ROWS), b
        )

    @pl.loop(0, ROWS - 1)
    def _(d):
        first_copy(d).start()

    orb_all[pl.ds(4 * a, 4)] = orb_mine[...]

    def vec_row_copy(d):
        col = lax.rem(b + 4 * (d + 1), COLS)
        return remote(vec_ref, vec_row.at[group], sva.at[d], rva.at[d], a, col)

    def vec_row_local():
        return pltpu.make_async_copy(vec_ref, vec_row.at[group], lva)

    @pl.loop(0, NK)
    def _(wanted):
        found = jnp.int32(0)
        for k in range(NK):
            found = jnp.where(value[k] == wanted, k, found)
        place[wanted] = found

    @pl.loop(0, ROWS - 1)
    def _(d):
        first_copy(d).wait()

    @pl.loop(0, COLS)
    def _(dest):
        for m in range(4):
            staged[dest, m] = orb_all[place[a + 8 * m]]
        for t in range(2):
            staged[dest, 4 + t] = orb_all[place[column_value(dest, t)]]

    def second_copy(d):
        col = lax.rem(b + d + 1, COLS)
        return remote(staged.at[col], landed.at[b], s2.at[d], r2.at[d], a, col)

    @pl.loop(0, COLS - 1)
    def _(d):
        second_copy(d).start()

    landed[b] = staged[b]

    residue = lax.rem(4 * lax.rem(a, 2) + group, 8)
    piece = level * 4 + quarter
    needed = lax.rem(a - chip + 8, 8)

    def screen_target(i):
        row = 2 * lax.rem(level - i // 2 + 4, 4) + lax.rem(i, 2)
        return row, 2 * lax.rem(row - residue + 8, 8) + core

    def screen_copy(i):
        row, col = screen_target(i)
        return remote(screen_ref, screen.at[piece], sw.at[i], rw.at[piece], row, col)

    def screen_local():
        return pltpu.make_async_copy(screen_ref, screen.at[piece], lw)

    def screen_self(i):
        row, col = screen_target(i)
        return jnp.logical_and(row == a, col == b)

    def forward_copy(p):
        return remote(screen.at[p], screen.at[p], sf.at[p], rw.at[p], a, b + 1 - 2 * core)

    @pl.loop(0, 8)
    def _(i):
        @pl.when(screen_self(i))
        def _():
            screen_local().start()

        @pl.when(jnp.logical_not(screen_self(i)))
        def _():
            screen_copy(i).start()

    for d in range(3):
        vec_row_copy(d).start()
    vec_row_local().start()

    def arrive(slot):
        for half in range(2):
            p = slot * 4 + core + 2 * half
            here = jnp.logical_and(needed == residue, p == piece)

            @pl.when(here)
            def _():
                screen_local().wait()

            @pl.when(jnp.logical_not(here))
            def _():
                remote(screen_ref, screen.at[p], sw.at[0], rw.at[p], lax.rem(a + 1, ROWS), b).wait_recv()

            forward_copy(p).start()

    def forwarded(slot):
        for half in range(2):
            p = slot * 4 + 1 - core + 2 * half
            forward_copy(p).wait_recv()

    @pl.loop(0, 8)
    def _(i):
        row = lax.broadcasted_iota(jnp.int32, (128, PAIRS), 0) + i * 128
        col = lax.broadcasted_iota(jnp.int32, (128, PAIRS), 1)
        hit = jnp.logical_and((row & 31) == (col >> 5), (row >> 5) == (col & 31))
        swap[pl.ds(pl.multiple_of(i * 128, 128), 128)] = jnp.where(hit, 1.0, 0.0).astype(jnp.bfloat16)

    point = place[a + 8 * group]
    lane = lax.broadcasted_iota(jnp.int32, (8, QUART), 1)
    upper = jnp.zeros((8, QUART), jnp.float32)
    lower = jnp.zeros((8, QUART), jnp.float32)
    for c in range(NC):
        upper = jnp.where((lane & 31) == c, energy[point, NV + c], upper)
    for v in range(8):
        lower = jnp.where((lane >> 5) == v, energy[point, 8 * quarter + v], lower)
    gap[...] = upper - lower

    @pl.loop(0, COLS - 1)
    def _(d):
        second_copy(d).wait()

    @pl.loop(0, 6)
    def _(slot):
        for source in range(COLS):
            wide[source * 16 : source * 16 + 16] = landed[source, slot].astype(jnp.float32)
        for part in range(4):
            orb[slot, :, part * 128 : part * 128 + 128] = wide[pl.ds(part, 64, stride=4), :]

    def vec_cross_copy(d):
        return remote(
            vec_sent.at[d], vec_got.at[a], svb.at[d], rvb.at[d], lax.rem(a + d + 1, ROWS), b
        )

    def turn_copy(step, source):
        return remote(
            source, passed.at[step], st.at[step], rt.at[step], chip, 2 * a + core
        )

    def turn_local(step, source):
        return pltpu.make_async_copy(source, passed.at[step], lt.at[step])

    def turn_start(step, source):
        @pl.when(chip == a)
        def _():
            turn_local(step, source).start()

        @pl.when(chip != a)
        def _():
            turn_copy(step, source).start()

    part_index = (a // 4) * 4 + 2 * lax.rem(a, 2) + core
    spread_col = 2 * chip + lax.rem(a // 2, 2)

    def spread_self(i):
        return jnp.logical_and(i == 0, spread_col == b)

    def spread_copy(step, i):
        return remote(
            passed.at[step],
            column.at[step, part_index],
            sg.at[step, i],
            rg.at[step, part_index],
            lax.rem(a + i, ROWS),
            spread_col,
        )

    def spread_local(step, p):
        return pltpu.make_async_copy(passed.at[step], column.at[step, p], lg.at[step])

    def spread_start(step, source):
        @pl.when(chip == a)
        def _():
            turn_local(step, source).wait()

        @pl.when(chip != a)
        def _():
            turn_copy(step, source).wait()

        @pl.loop(0, ROWS)
        def _(i):
            @pl.when(spread_self(i))
            def _():
                spread_local(step, part_index).start()

            @pl.when(jnp.logical_not(spread_self(i)))
            def _():
                spread_copy(step, i).start()

    def spread_wait(step):
        @pl.loop(0, 8)
        def _(p):
            here = jnp.logical_and(spread_col == b, p == part_index)

            @pl.when(here)
            def _():
                spread_local(step, p).wait()

            @pl.when(jnp.logical_not(here))
            def _():
                remote(
                    passed.at[step],
                    column.at[step, p],
                    sg.at[step, 0],
                    rg.at[step, p],
                    lax.rem(a + 1, ROWS),
                    b,
                ).wait_recv()

    wrap = jnp.where(a >= chip, 0, 1)
    lane = lax.broadcasted_iota(jnp.int32, (32, 128), 1)
    low = lane < 64
    even = (lane & 32) == 0

    def build(slot, m, t):
        left, right = m, 4 + t
        for v in range(NV):
            valence[v * 32 : v * 32 + 32] = (orb[left, v : v + 1] * orb[right, :NV]).astype(jnp.bfloat16)
            conduct[v * 32 : v * 32 + 32] = (orb[right, NV + v : NV + v + 1] * orb[left, NV:]).astype(
                jnp.bfloat16
            )
        block = screen[pl.ds(slot * 4, 4)].reshape(NG, NG)
        amplitude[...] = jnp.dot(valence[...], block, preferred_element_type=jnp.float32).astype(jnp.bfloat16)
        for block in range(4):
            product[...] = lax.dot_general(
                amplitude[...],
                conduct[block * 256 : block * 256 + 256],
                (((1,), (1,)), ((), ())),
                preferred_element_type=jnp.float32,
            )
            for octet in range(8):
                for half in range(2):
                    s = [
                        product[octet * 128 + i * 32 : octet * 128 + i * 32 + 32, half * 128 : half * 128 + 128]
                        for i in range(4)
                    ]
                    u0 = jnp.where(low, s[0], pltpu.roll(s[2], 64, 1))
                    u2 = jnp.where(low, pltpu.roll(s[0], 64, 1), s[2])
                    u1 = jnp.where(low, s[1], pltpu.roll(s[3], 64, 1))
                    u3 = jnp.where(low, pltpu.roll(s[1], 64, 1), s[3])
                    turned = [
                        jnp.where(even, u0, pltpu.roll(u1, 32, 1)),
                        jnp.where(even, pltpu.roll(u0, 96, 1), u1),
                        jnp.where(even, u2, pltpu.roll(u3, 32, 1)),
                        jnp.where(even, pltpu.roll(u2, 96, 1), u3),
                    ]
                    first = block * 256 + half * 128
                    lanes = (octet % 2) * 128
                    for i in range(4):
                        tiles[m, octet // 2, t, first + i * 32 : first + i * 32 + 32, lanes : lanes + 128] = turned[
                            i
                        ].astype(jnp.bfloat16)

    arrive(level)

    @pl.loop(0, 4)
    def _(phase):
        slot = lax.rem(level + phase, 4)

        @pl.when(phase < 3)
        def _():
            arrive(lax.rem(slot + 1, 4))

        forwarded(slot)

        @pl.loop(0, 2)
        def _(t):
            build(slot, lax.rem(slot + wrap + core + 2 * t, 4), t)

        @pl.when(phase == 0)
        def _():
            for d in range(3):
                vec_row_copy(d).wait()
            vec_row_local().wait()
            for d in range(7):
                home = lax.rem(a + d + 1, ROWS) + 8 * group
                vec_sent[d] = vec_row[lax.rem(place[home], 4)]
                vec_cross_copy(d).start()
            vec_got[a] = vec_row[lax.rem(place[a + 8 * group], 4)]

        @pl.when(phase == 1)
        def _():
            for d in range(7):
                vec_cross_copy(d).wait()
            own[...] = vec_got[place[a + 8 * group] // 4]
            turn_start(0, own)

        @pl.when(phase == 2)
        def _():
            spread_start(0, own)

    @pl.loop(0, 8)
    def _(i):
        @pl.when(jnp.logical_not(screen_self(i)))
        def _():
            screen_copy(i).wait_send()

    for slot in range(4):
        for half in range(2):
            forward_copy(slot * 4 + core + 2 * half).wait_send()

    mine = own[...].astype(jnp.float32)
    levels = gap[0:1]

    def partial_copy(step, col):
        return remote(sent.at[step, col], got.at[step, b], sp.at[step, col], rp.at[step, b], a, col)

    def partial_arrival(step, source):
        return remote(sent.at[step, source], got.at[step, source], sp.at[step, source], rp.at[step, source], a, source)

    for step in range(3):
        spread_wait(step)
        for t in range(2):
            turned = jnp.zeros((NX, PAIRS), jnp.float32)
            for j in range(4):
                turned += jnp.dot(
                    column[step, t * 4 + j],
                    swap[j * QUART : j * QUART + QUART],
                    preferred_element_type=jnp.float32,
                )
            ordered[:, t * PAIRS : t * PAIRS + PAIRS] = turned.astype(jnp.bfloat16)

        @pl.loop(0, 4)
        def _(i):
            m = lax.rem(group + 1 + i, 4)
            for j in range(4):
                col = 4 * m + j
                sent[step, col] = jnp.dot(
                    ordered[...],
                    tiles[m, j].reshape(2 * PAIRS, QUART),
                    preferred_element_type=jnp.float32,
                ).astype(jnp.bfloat16)

                @pl.when(col != b)
                def _():
                    partial_copy(step, col).start()

        got[step, b] = sent[step, b]

        @pl.loop(0, COLS - 1)
        def _(d):
            source = lax.rem(b + d + 1, COLS)
            partial_arrival(step, source).wait_recv()

        total = jnp.zeros((NX, QUART), jnp.float32)
        for source in range(COLS):
            total += got[step, source].astype(jnp.float32)
        if step == 0:
            new = (levels * mine + total) / SPREAD
            state[0] = new
        elif step == 1:
            new = 2.0 * ((levels * state[0] + total) / SPREAD) - mine
            state[1] = new
        else:
            new = 2.0 * ((levels * state[1] + total) / SPREAD) - state[0]
        if step < 2:
            rounded[step] = new.astype(jnp.bfloat16)
            turn_start(step + 1, rounded.at[step])
            spread_start(step + 1, rounded.at[step])
        else:
            final_row[group] = new

    def row_copy(d):
        col = lax.rem(b + 4 * (d + 1), COLS)
        return remote(final_row.at[group], final_row.at[group], sa.at[d], ra.at[d], a, col)

    for d in range(3):
        row_copy(d).start()

    for step in range(3):

        @pl.loop(0, ROWS)
        def _(i):
            @pl.when(jnp.logical_not(spread_self(i)))
            def _():
                spread_copy(step, i).wait_send()

        @pl.loop(0, COLS - 1)
        def _(d):
            partial_copy(step, lax.rem(b + d + 1, COLS)).wait_send()

    for d in range(3):
        row_copy(d).wait()

    def last_copy(d):
        return remote(final_sent.at[d], final_got.at[a], sb.at[d], rb.at[d], lax.rem(a + d + 1, ROWS), b)

    for d in range(7):
        final_sent[d] = final_row[value[4 * lax.rem(a + d + 1, ROWS) + group] // 8]
        last_copy(d).start()
    final_got[a] = final_row[value[4 * a + group] // 8]
    for d in range(7):
        last_copy(d).wait()
    out_ref[...] = final_got[lax.rem(value[4 * a + group], 8)]


def per_device(orbitals, screened, kpoints, vectors, energies):
    dma = pltpu.SemaphoreType.DMA
    vmem = pl.BlockSpec(memory_space=pltpu.VMEM)
    smem = pl.BlockSpec(memory_space=pltpu.SMEM)
    anywhere = pl.BlockSpec(memory_space=pl.ANY)
    half, full = jnp.bfloat16, jnp.float32
    return pl.pallas_call(
        kernel,
        out_shape=jax.ShapeDtypeStruct((NX, QUART), full),
        in_specs=[smem, smem, vmem, anywhere, anywhere],
        out_specs=vmem,
        scratch_shapes=[
            pltpu.SMEM((NK,), jnp.int32),
            pltpu.VMEM((256, 128), full),
            pltpu.VMEM((4, 16, 128), half),
            pltpu.VMEM((NK, 16, 128), half),
            pltpu.VMEM((COLS, 6, 16, 128), half),
            pltpu.VMEM((COLS, 6, 16, 128), half),
            pltpu.VMEM((6, 64, NG), full),
            pltpu.VMEM((16, 128, NG), half),
            pltpu.VMEM((PAIRS, NG), half),
            pltpu.VMEM((PAIRS, NG), half),
            pltpu.VMEM((PAIRS, NG), half),
            pltpu.VMEM((PAIRS, 256), full),
            pltpu.VMEM((4, 4, 2, PAIRS, QUART), half),
            pltpu.VMEM((PAIRS, PAIRS), half),
            pltpu.VMEM((4, NX, QUART), half),
            pltpu.VMEM((7, NX, QUART), half),
            pltpu.VMEM((8, NX, QUART), half),
            pltpu.VMEM((NX, QUART), half),
            pltpu.VMEM((8, QUART), full),
            pltpu.VMEM((3, NX, QUART), half),
            pltpu.VMEM((3, 8, NX, QUART), half),
            pltpu.VMEM((NX, 2 * PAIRS), half),
            pltpu.VMEM((3, COLS, NX, QUART), half),
            pltpu.VMEM((3, COLS, NX, QUART), half),
            pltpu.VMEM((2, NX, QUART), half),
            pltpu.VMEM((2, NX, QUART), full),
            pltpu.VMEM((4, NX, QUART), full),
            pltpu.VMEM((7, NX, QUART), full),
            pltpu.VMEM((8, NX, QUART), full),
            dma((7,)),
            dma((7,)),
            dma((15,)),
            dma((15,)),
            dma((8,)),
            dma((16,)),
            dma,
            dma((16,)),
            dma((3,)),
            dma((3,)),
            dma,
            dma((7,)),
            dma((7,)),
            dma((3,)),
            dma((3,)),
            dma((3,)),
            dma((3, 8)),
            dma((3, 8)),
            dma((3,)),
            dma((3, 16)),
            dma((3, 16)),
            dma((3,)),
            dma((3,)),
            dma((7,)),
            dma((7,)),
        ],
        compiler_params=pltpu.CompilerParams(has_side_effects=True, vmem_limit_bytes=56 << 20),
        name="mega",
    )(kpoints, energies, orbitals, screened, vectors)


def solution(mesh):
    placed = (P("row", "col", None), P(("row", "col"), None), P(), P(None, ("row", "col")), P())
    return jax.shard_map(
        per_device, mesh=mesh, in_specs=placed, out_specs=P(None, ("row", "col")), check_vma=False
    )
```

```python
import jax
import jax.numpy as jnp
from jax import lax
from jax.experimental import pallas as pl
from jax.experimental.pallas import tpu as pltpu
from jax.sharding import PartitionSpec as P

NV = 32
NC = 32
NG = 512
NX = 64
NK = 32
PAIRS = NV * NC
ROWS = 8
COLS = 16
SPREAD = 4.0
QUART = PAIRS // 4


def column_value(col, t):
    return col // 2 + 8 * lax.rem(col, 2) + 16 * t


def remote(src, dst, send_sem, recv_sem, row, col):
    return pltpu.make_async_remote_copy(
        src_ref=src,
        dst_ref=dst,
        send_sem=send_sem,
        recv_sem=recv_sem,
        device_id=(row, col),
        device_id_type=pl.DeviceIdType.MESH,
    )


def kernel(
    value,
    energy,
    orb_ref,
    screen_ref,
    vec_ref,
    out_ref,
    place,
    wide,
    orb_mine,
    orb_all,
    staged,
    landed,
    orb,
    screen,
    valence,
    conduct,
    amplitude,
    product,
    tiles,
    swap,
    vec_row,
    vec_sent,
    vec_got,
    own,
    gap,
    passed,
    column,
    ordered,
    sent,
    got,
    rounded,
    state,
    final_row,
    final_sent,
    final_got,
    s1,
    r1,
    s2,
    r2,
    sw,
    rw,
    lw,
    sf,
    sva,
    rva,
    lva,
    svb,
    rvb,
    st,
    rt,
    lt,
    sg,
    rg,
    lg,
    sp,
    rp,
    sa,
    ra,
    sb,
    rb,
):
    a = lax.axis_index("row")
    b = lax.axis_index("col")
    quarter = lax.rem(b, 4)
    group = b // 4
    chip = b // 2
    core = lax.rem(b, 2)
    level = a // 2
    residue = lax.rem(4 * lax.rem(a, 2) + group, 8)
    piece = level * 4 + quarter
    needed = lax.rem(a - chip + 8, 8)

    barrier = pltpu.get_barrier_semaphore()

    def greet(row, col):
        pl.semaphore_signal(barrier, inc=1, device_id=(row, col), device_id_type=pl.DeviceIdType.MESH)

    @pl.loop(0, ROWS - 1)
    def _(d):
        greet(lax.rem(a + d + 1, ROWS), b)

    @pl.loop(0, COLS - 1)
    def _(d):
        greet(a, lax.rem(b + d + 1, COLS))

    @pl.loop(0, 8)
    def _(i):
        row = 2 * (i // 2) + needed // 4
        col = 4 * lax.rem(needed, 4) + core + 2 * lax.rem(i, 2)

        @pl.when(jnp.logical_or(row != a, col != b))
        def _():
            greet(row, col)

    @pl.when(chip != a)
    def _():
        greet(chip, 2 * a + core)

    @pl.loop(0, 4)
    def _(i):
        greet(2 * core + lax.rem(i, 2) + 4 * (i // 2), b + 1 - 2 * core)

    peers = ROWS - 1 + COLS - 1 + 7
    peers += jnp.where(needed != residue, 1, 0)
    peers += jnp.where(chip != a, 1, 0)
    peers += jnp.where(lax.rem(level, 2) != core, 8, 0)
    pl.semaphore_wait(barrier, peers)

    for k in range(4):
        for part in range(4):
            wide[pl.ds(k * 16 + part, 4, stride=4), :] = orb_ref[k, :, part * 128 : part * 128 + 128].astype(
                jnp.float32
            )
    for k in range(4):
        orb_mine[k] = wide[k * 16 : k * 16 + 16].astype(jnp.bfloat16)

    def first_copy(d):
        return remote(
            orb_mine, orb_all.at[pl.ds(4 * a, 4)], s1.at[d], r1.at[d], lax.rem(a + d + 1, ROWS), b
        )

    @pl.loop(0, ROWS - 1)
    def _(d):
        first_copy(d).start()

    orb_all[pl.ds(4 * a, 4)] = orb_mine[...]

    def vec_row_copy(d):
        col = lax.rem(b + 4 * (d + 1), COLS)
        return remote(vec_ref, vec_row.at[group], sva.at[d], rva.at[d], a, col)

    def vec_row_local():
        return pltpu.make_async_copy(vec_ref, vec_row.at[group], lva)

    def screen_target(i):
        row = 2 * lax.rem(level - i // 2 + 4, 4) + lax.rem(i, 2)
        return row, 2 * lax.rem(row - residue + 8, 8) + core

    def screen_copy(i):
        row, col = screen_target(i)
        return remote(screen_ref, screen.at[piece], sw.at[i], rw.at[piece], row, col)

    def screen_local():
        return pltpu.make_async_copy(screen_ref, screen.at[piece], lw)

    def screen_self(i):
        row, col = screen_target(i)
        return jnp.logical_and(row == a, col == b)

    def forward_copy(p):
        return remote(screen.at[p], screen.at[p], sf.at[p], rw.at[p], a, b + 1 - 2 * core)

    @pl.loop(0, 8)
    def _(i):
        @pl.when(screen_self(i))
        def _():
            screen_local().start()

        @pl.when(jnp.logical_not(screen_self(i)))
        def _():
            screen_copy(i).start()

    @pl.loop(0, NK)
    def _(wanted):
        found = jnp.int32(0)
        for k in range(NK):
            found = jnp.where(value[k] == wanted, k, found)
        place[wanted] = found

    @pl.loop(0, ROWS - 1)
    def _(d):
        first_copy(d).wait()

    @pl.loop(0, COLS)
    def _(dest):
        for m in range(4):
            staged[dest, m] = orb_all[place[a + 8 * m]]
        for t in range(2):
            staged[dest, 4 + t] = orb_all[place[column_value(dest, t)]]

    def second_copy(d):
        col = lax.rem(b + d + 1, COLS)
        return remote(staged.at[col], landed.at[b], s2.at[d], r2.at[d], a, col)

    @pl.loop(0, COLS - 1)
    def _(d):
        second_copy(d).start()

    landed[b] = staged[b]

    for d in range(3):
        vec_row_copy(d).start()
    vec_row_local().start()

    def arrive(slot):
        for half in range(2):
            p = slot * 4 + core + 2 * half
            here = jnp.logical_and(needed == residue, p == piece)

            @pl.when(here)
            def _():
                screen_local().wait()

            @pl.when(jnp.logical_not(here))
            def _():
                remote(screen_ref, screen.at[p], sw.at[0], rw.at[p], lax.rem(a + 1, ROWS), b).wait_recv()

            forward_copy(p).start()

    def forwarded(slot):
        for half in range(2):
            p = slot * 4 + 1 - core + 2 * half
            forward_copy(p).wait_recv()

    @pl.loop(0, 8)
    def _(i):
        row = lax.broadcasted_iota(jnp.int32, (128, PAIRS), 0) + i * 128
        col = lax.broadcasted_iota(jnp.int32, (128, PAIRS), 1)
        hit = jnp.logical_and((row & 31) == (col >> 5), (row >> 5) == (col & 31))
        swap[pl.ds(pl.multiple_of(i * 128, 128), 128)] = jnp.where(hit, 1.0, 0.0).astype(jnp.bfloat16)

    point = place[a + 8 * group]
    lane = lax.broadcasted_iota(jnp.int32, (8, QUART), 1)
    upper = jnp.zeros((8, QUART), jnp.float32)
    lower = jnp.zeros((8, QUART), jnp.float32)
    for c in range(NC):
        upper = jnp.where((lane & 31) == c, energy[point, NV + c], upper)
    for v in range(8):
        lower = jnp.where((lane >> 5) == v, energy[point, 8 * quarter + v], lower)
    gap[...] = upper - lower

    @pl.loop(0, COLS - 1)
    def _(d):
        second_copy(d).wait()

    @pl.loop(0, 6)
    def _(slot):
        for source in range(COLS):
            wide[source * 16 : source * 16 + 16] = landed[source, slot].astype(jnp.float32)
        for part in range(4):
            orb[slot, :, part * 128 : part * 128 + 128] = wide[pl.ds(part, 64, stride=4), :]

    def vec_cross_copy(d):
        return remote(
            vec_sent.at[d], vec_got.at[a], svb.at[d], rvb.at[d], lax.rem(a + d + 1, ROWS), b
        )

    def turn_copy(step, source):
        return remote(
            source, passed.at[step], st.at[step], rt.at[step], chip, 2 * a + core
        )

    def turn_local(step, source):
        return pltpu.make_async_copy(source, passed.at[step], lt.at[step])

    def turn_start(step, source):
        @pl.when(chip == a)
        def _():
            turn_local(step, source).start()

        @pl.when(chip != a)
        def _():
            turn_copy(step, source).start()

    part_index = (a // 4) * 4 + 2 * lax.rem(a, 2) + core
    spread_col = 2 * chip + lax.rem(a // 2, 2)

    def spread_self(i):
        return jnp.logical_and(i == 0, spread_col == b)

    def spread_copy(step, i):
        return remote(
            passed.at[step],
            column.at[step, part_index],
            sg.at[step, i],
            rg.at[step, part_index],
            lax.rem(a + i, ROWS),
            spread_col,
        )

    def spread_local(step, p):
        return pltpu.make_async_copy(passed.at[step], column.at[step, p], lg.at[step])

    def spread_start(step, source):
        @pl.when(chip == a)
        def _():
            turn_local(step, source).wait()

        @pl.when(chip != a)
        def _():
            turn_copy(step, source).wait()

        @pl.loop(0, ROWS)
        def _(i):
            @pl.when(spread_self(i))
            def _():
                spread_local(step, part_index).start()

            @pl.when(jnp.logical_not(spread_self(i)))
            def _():
                spread_copy(step, i).start()

    def spread_wait(step):
        @pl.loop(0, 8)
        def _(p):
            here = jnp.logical_and(spread_col == b, p == part_index)

            @pl.when(here)
            def _():
                spread_local(step, p).wait()

            @pl.when(jnp.logical_not(here))
            def _():
                remote(
                    passed.at[step],
                    column.at[step, p],
                    sg.at[step, 0],
                    rg.at[step, p],
                    lax.rem(a + 1, ROWS),
                    b,
                ).wait_recv()

    wrap = jnp.where(a >= chip, 0, 1)
    lane = lax.broadcasted_iota(jnp.int32, (32, 128), 1)
    low = lane < 64
    even = (lane & 32) == 0

    def build(slot, m, t):
        left, right = m, 4 + t
        for v in range(NV):
            valence[v * 32 : v * 32 + 32] = (orb[left, v : v + 1] * orb[right, :NV]).astype(jnp.bfloat16)
            conduct[v * 32 : v * 32 + 32] = (orb[right, NV + v : NV + v + 1] * orb[left, NV:]).astype(
                jnp.bfloat16
            )
        block = screen[pl.ds(slot * 4, 4)].reshape(NG, NG)
        amplitude[...] = jnp.dot(valence[...], block, preferred_element_type=jnp.float32).astype(jnp.bfloat16)
        for block in range(4):
            product[...] = lax.dot_general(
                amplitude[...],
                conduct[block * 256 : block * 256 + 256],
                (((1,), (1,)), ((), ())),
                preferred_element_type=jnp.float32,
            )
            for octet in range(8):
                for half in range(2):
                    s = [
                        product[octet * 128 + i * 32 : octet * 128 + i * 32 + 32, half * 128 : half * 128 + 128]
                        for i in range(4)
                    ]
                    u0 = jnp.where(low, s[0], pltpu.roll(s[2], 64, 1))
                    u2 = jnp.where(low, pltpu.roll(s[0], 64, 1), s[2])
                    u1 = jnp.where(low, s[1], pltpu.roll(s[3], 64, 1))
                    u3 = jnp.where(low, pltpu.roll(s[1], 64, 1), s[3])
                    turned = [
                        jnp.where(even, u0, pltpu.roll(u1, 32, 1)),
                        jnp.where(even, pltpu.roll(u0, 96, 1), u1),
                        jnp.where(even, u2, pltpu.roll(u3, 32, 1)),
                        jnp.where(even, pltpu.roll(u2, 96, 1), u3),
                    ]
                    first = block * 256 + half * 128
                    lanes = (octet % 2) * 128
                    for i in range(4):
                        tiles[m, octet // 2, t, first + i * 32 : first + i * 32 + 32, lanes : lanes + 128] = turned[
                            i
                        ].astype(jnp.bfloat16)

    arrive(level)

    @pl.loop(0, 4)
    def _(phase):
        slot = lax.rem(level + phase, 4)

        @pl.when(phase < 3)
        def _():
            arrive(lax.rem(slot + 1, 4))

        forwarded(slot)

        @pl.loop(0, 2)
        def _(t):
            build(slot, lax.rem(slot + wrap + core + 2 * t, 4), t)

        @pl.when(phase == 0)
        def _():
            for d in range(3):
                vec_row_copy(d).wait()
            vec_row_local().wait()
            for d in range(7):
                home = lax.rem(a + d + 1, ROWS) + 8 * group
                vec_sent[d] = vec_row[lax.rem(place[home], 4)]
                vec_cross_copy(d).start()
            vec_got[a] = vec_row[lax.rem(place[a + 8 * group], 4)]

        @pl.when(phase == 1)
        def _():
            for d in range(7):
                vec_cross_copy(d).wait()
            own[...] = vec_got[place[a + 8 * group] // 4]
            turn_start(0, own)

        @pl.when(phase == 2)
        def _():
            spread_start(0, own)

    @pl.loop(0, 8)
    def _(i):
        @pl.when(jnp.logical_not(screen_self(i)))
        def _():
            screen_copy(i).wait_send()

    for slot in range(4):
        for half in range(2):
            forward_copy(slot * 4 + core + 2 * half).wait_send()

    mine = own[...].astype(jnp.float32)
    levels = gap[0:1]

    def partial_copy(step, col):
        return remote(sent.at[step, col], got.at[step, b], sp.at[step, col], rp.at[step, b], a, col)

    def partial_arrival(step, source):
        return remote(sent.at[step, source], got.at[step, source], sp.at[step, source], rp.at[step, source], a, source)

    for step in range(3):
        spread_wait(step)
        for t in range(2):
            turned = jnp.zeros((NX, PAIRS), jnp.float32)
            for j in range(4):
                turned += jnp.dot(
                    column[step, t * 4 + j],
                    swap[j * QUART : j * QUART + QUART],
                    preferred_element_type=jnp.float32,
                )
            ordered[:, t * PAIRS : t * PAIRS + PAIRS] = turned.astype(jnp.bfloat16)

        @pl.loop(0, 4)
        def _(i):
            m = lax.rem(group + 1 + i, 4)
            for j in range(4):
                col = 4 * m + j
                sent[step, col] = jnp.dot(
                    ordered[...],
                    tiles[m, j].reshape(2 * PAIRS, QUART),
                    preferred_element_type=jnp.float32,
                ).astype(jnp.bfloat16)

                @pl.when(col != b)
                def _():
                    partial_copy(step, col).start()

        got[step, b] = sent[step, b]

        @pl.loop(0, COLS - 1)
        def _(d):
            source = lax.rem(b + d + 1, COLS)
            partial_arrival(step, source).wait_recv()

        total = jnp.zeros((NX, QUART), jnp.float32)
        for source in range(COLS):
            total += got[step, source].astype(jnp.float32)
        if step == 0:
            new = (levels * mine + total) / SPREAD
            state[0] = new
        elif step == 1:
            new = 2.0 * ((levels * state[0] + total) / SPREAD) - mine
            state[1] = new
        else:
            new = 2.0 * ((levels * state[1] + total) / SPREAD) - state[0]
        if step < 2:
            rounded[step] = new.astype(jnp.bfloat16)
            turn_start(step + 1, rounded.at[step])
            spread_start(step + 1, rounded.at[step])
        else:
            final_row[group] = new.astype(jnp.bfloat16)

    def row_copy(d):
        col = lax.rem(b + 4 * (d + 1), COLS)
        return remote(final_row.at[group], final_row.at[group], sa.at[d], ra.at[d], a, col)

    for d in range(3):
        row_copy(d).start()

    for step in range(3):

        @pl.loop(0, ROWS)
        def _(i):
            @pl.when(jnp.logical_not(spread_self(i)))
            def _():
                spread_copy(step, i).wait_send()

        @pl.loop(0, COLS - 1)
        def _(d):
            partial_copy(step, lax.rem(b + d + 1, COLS)).wait_send()

    for d in range(3):
        row_copy(d).wait()

    def last_copy(d):
        return remote(final_sent.at[d], final_got.at[a], sb.at[d], rb.at[d], lax.rem(a + d + 1, ROWS), b)

    for d in range(7):
        final_sent[d] = final_row[value[4 * lax.rem(a + d + 1, ROWS) + group] // 8]
        last_copy(d).start()
    final_got[a] = final_row[value[4 * a + group] // 8]
    for d in range(7):
        last_copy(d).wait()
    out_ref[...] = final_got[lax.rem(value[4 * a + group], 8)].astype(jnp.float32)


def per_device(orbitals, screened, kpoints, vectors, energies):
    dma = pltpu.SemaphoreType.DMA
    vmem = pl.BlockSpec(memory_space=pltpu.VMEM)
    smem = pl.BlockSpec(memory_space=pltpu.SMEM)
    anywhere = pl.BlockSpec(memory_space=pl.ANY)
    half, full = jnp.bfloat16, jnp.float32
    return pl.pallas_call(
        kernel,
        out_shape=jax.ShapeDtypeStruct((NX, QUART), full),
        in_specs=[smem, smem, vmem, anywhere, anywhere],
        out_specs=vmem,
        scratch_shapes=[
            pltpu.SMEM((NK,), jnp.int32),
            pltpu.VMEM((256, 128), full),
            pltpu.VMEM((4, 16, 128), half),
            pltpu.VMEM((NK, 16, 128), half),
            pltpu.VMEM((COLS, 6, 16, 128), half),
            pltpu.VMEM((COLS, 6, 16, 128), half),
            pltpu.VMEM((6, 64, NG), full),
            pltpu.VMEM((16, 128, NG), half),
            pltpu.VMEM((PAIRS, NG), half),
            pltpu.VMEM((PAIRS, NG), half),
            pltpu.VMEM((PAIRS, NG), half),
            pltpu.VMEM((PAIRS, 256), full),
            pltpu.VMEM((4, 4, 2, PAIRS, QUART), half),
            pltpu.VMEM((PAIRS, PAIRS), half),
            pltpu.VMEM((4, NX, QUART), half),
            pltpu.VMEM((7, NX, QUART), half),
            pltpu.VMEM((8, NX, QUART), half),
            pltpu.VMEM((NX, QUART), half),
            pltpu.VMEM((8, QUART), full),
            pltpu.VMEM((3, NX, QUART), half),
            pltpu.VMEM((3, 8, NX, QUART), half),
            pltpu.VMEM((NX, 2 * PAIRS), half),
            pltpu.VMEM((3, COLS, NX, QUART), half),
            pltpu.VMEM((3, COLS, NX, QUART), half),
            pltpu.VMEM((2, NX, QUART), half),
            pltpu.VMEM((2, NX, QUART), full),
            pltpu.VMEM((4, NX, QUART), half),
            pltpu.VMEM((7, NX, QUART), half),
            pltpu.VMEM((8, NX, QUART), half),
            dma((7,)),
            dma((7,)),
            dma((15,)),
            dma((15,)),
            dma((8,)),
            dma((16,)),
            dma,
            dma((16,)),
            dma((3,)),
            dma((3,)),
            dma,
            dma((7,)),
            dma((7,)),
            dma((3,)),
            dma((3,)),
            dma((3,)),
            dma((3, 8)),
            dma((3, 8)),
            dma((3,)),
            dma((3, 16)),
            dma((3, 16)),
            dma((3,)),
            dma((3,)),
            dma((7,)),
            dma((7,)),
        ],
        compiler_params=pltpu.CompilerParams(
            has_side_effects=True, collective_id=0, vmem_limit_bytes=56 << 20),
        name="mega",
    )(kpoints, energies, orbitals, screened, vectors)


def solution(mesh):
    placed = (P("row", "col", None), P(("row", "col"), None), P(), P(None, ("row", "col")), P())
    return jax.shard_map(
        per_device, mesh=mesh, in_specs=placed, out_specs=P(None, ("row", "col")), check_vma=False
    )
```

```python
import jax
import jax.numpy as jnp
from jax import lax
from jax.experimental import pallas as pl
from jax.experimental.pallas import tpu as pltpu
from jax.sharding import PartitionSpec as P

NV = 32
NC = 32
NG = 512
NX = 64
NK = 32
PAIRS = NV * NC
ROWS = 8
COLS = 16
SPREAD = 4.0
QUART = PAIRS // 4


def labels(row, col):
    x, y, z = lax.rem(col, 8) // 2, 2 * (col // 8) + lax.rem(row, 2), row // 2
    alpha = 4 * (z // 2) + 2 * lax.rem((y + 1) // 2, 2) + x // 2
    beta = 4 * lax.rem((z + 1) // 2, 2) + 2 * (y // 2) + lax.rem((x + 1) // 2, 2)
    return alpha, beta


def device(alpha, beta, core):
    ax, ay, az = lax.rem(alpha, 2), lax.rem(alpha // 2, 2), alpha // 4
    bx, by, bz = lax.rem(beta, 2), lax.rem(beta // 2, 2), beta // 4
    x = bx + ax * (3 - 2 * bx)
    y = ay + by * (3 - 2 * ay)
    z = bz + az * (3 - 2 * bz)
    return 2 * z + lax.rem(y, 2), 8 * (y // 2) + 2 * x + core


def order_of(beta):
    return 4 * lax.rem(beta // 2, 2) + 2 * (beta // 4) + lax.rem(beta // 4 + beta, 2)


def beta_of(order):
    high = lax.rem(order // 2, 2)
    return 4 * high + 2 * (order // 4) + lax.rem(order + high, 2)


def remote(src, dst, send_sem, recv_sem, row, col):
    return pltpu.make_async_remote_copy(
        src_ref=src,
        dst_ref=dst,
        send_sem=send_sem,
        recv_sem=recv_sem,
        device_id=(row, col),
        device_id_type=pl.DeviceIdType.MESH,
    )


def kernel(
    value,
    energy,
    orb_ref,
    screen_ref,
    vec_ref,
    out_ref,
    place,
    wide,
    orb_mine,
    orb_all,
    staged,
    landed,
    orb,
    screen,
    valence,
    conduct,
    amplitude,
    product,
    tiles,
    swap,
    vec_row,
    vec_sent,
    vec_got,
    own,
    gap,
    passed,
    column,
    ordered,
    sent,
    got,
    rounded,
    state,
    final_row,
    final_sent,
    final_got,
    s1,
    r1,
    s2,
    r2,
    sw,
    rw,
    lw,
    sf,
    sva,
    rva,
    lva,
    svb,
    rvb,
    st,
    rt,
    sg,
    rg,
    lg,
    sp,
    rp,
    sa,
    ra,
    sb,
    rb,
    lb,
):
    a = lax.axis_index("row")
    b = lax.axis_index("col")
    core = lax.rem(b, 2)
    alpha, beta = labels(a, b)
    order = order_of(beta)
    level = a // 2
    part = lax.rem(b, 4)
    residue = 4 * lax.rem(a, 2) + b // 4
    piece = level * 4 + part
    needed = lax.rem(alpha - beta + 8, 8)
    group = order // 2
    quarter = 2 * lax.rem(order, 2) + core
    point_value = alpha + 8 * group
    me = 2 * order + core

    def peer(index):
        return device(alpha, beta_of(index // 2), lax.rem(index, 2))

    barrier = pltpu.get_barrier_semaphore()

    @pl.loop(1, ROWS * COLS)
    def _(d):
        other = lax.rem(a * COLS + b + d, ROWS * COLS)
        pl.semaphore_signal(
            barrier,
            inc=1,
            device_id=(other // COLS, lax.rem(other, COLS)),
            device_id_type=pl.DeviceIdType.MESH,
        )

    pl.semaphore_wait(barrier, ROWS * COLS - 1)

    for k in range(4):
        for lanes in range(4):
            wide[pl.ds(k * 16 + lanes, 4, stride=4), :] = orb_ref[k, :, lanes * 128 : lanes * 128 + 128].astype(
                jnp.float32
            )
    for k in range(4):
        orb_mine[k] = wide[k * 16 : k * 16 + 16].astype(jnp.bfloat16)

    def first_copy(d):
        return remote(
            orb_mine, orb_all.at[pl.ds(4 * a, 4)], s1.at[d], r1.at[d], lax.rem(a + d + 1, ROWS), b
        )

    @pl.loop(0, ROWS - 1)
    def _(d):
        first_copy(d).start()

    orb_all[pl.ds(4 * a, 4)] = orb_mine[...]

    vec_self = b // 2 == order

    def vec_first_copy(label):
        row, col = device(label, beta_of(b // 2), core)
        return remote(vec_ref, vec_got.at[a], sva.at[label], rva.at[a], row, col)

    def vec_first_local():
        return pltpu.make_async_copy(vec_ref, vec_got.at[a], lva)

    def screen_target(label):
        return device(label, lax.rem(label - residue + 8, 8), core)

    def screen_copy(i):
        row, col = screen_target(i)
        return remote(screen_ref, screen.at[piece], sw.at[i], rw.at[piece], row, col)

    def screen_local():
        return pltpu.make_async_copy(screen_ref, screen.at[piece], lw)

    def screen_self(i):
        row, col = screen_target(i)
        return jnp.logical_and(row == a, col == b)

    def forward_copy(p):
        return remote(screen.at[p], screen.at[p], sf.at[p], rw.at[p], a, b + 1 - 2 * core)

    @pl.loop(0, 32)
    def _(i):
        label = lax.rem(i + alpha, 8)
        turn = lax.rem(level - screen_target(label)[0] // 2 + 4, 4) == i // 8

        @pl.when(jnp.logical_and(turn, screen_self(label)))
        def _():
            screen_local().start()

        @pl.when(jnp.logical_and(turn, jnp.logical_not(screen_self(label))))
        def _():
            screen_copy(label).start()

    @pl.loop(0, NK)
    def _(wanted):
        found = jnp.int32(0)
        for k in range(NK):
            found = jnp.where(value[k] == wanted, k, found)
        place[wanted] = found

    @pl.loop(0, ROWS - 1)
    def _(d):
        first_copy(d).wait()

    def second_target(col):
        return jnp.where(col // 8 == b // 8, a, a + 1 - 2 * lax.rem(a, 2)), col

    @pl.loop(0, COLS)
    def _(dest):
        row, col = second_target(dest)
        alpha_there, beta_there = labels(row, col)
        for m in range(4):
            staged[dest, m] = orb_all[place[alpha_there + 8 * m]]
        for t in range(2):
            staged[dest, 4 + t] = orb_all[place[beta_there + 8 * lax.rem(col, 2) + 16 * t]]

    def second_copy(d):
        row, col = second_target(lax.rem(b + d + 1, COLS))
        return remote(staged.at[col], landed.at[b], s2.at[d], r2.at[d], row, col)

    @pl.loop(0, COLS - 1)
    def _(d):
        second_copy(d).start()

    landed[b] = staged[b]

    def vec_start():
        @pl.loop(0, 8)
        def _(i):
            label = lax.rem(i + alpha, 8)
            here = jnp.logical_and(vec_self, label == alpha)

            @pl.when(here)
            def _():
                vec_first_local().start()

            @pl.when(jnp.logical_not(here))
            def _():
                vec_first_copy(label).start()

    def arrive(slot):
        for half in range(2):
            p = slot * 4 + core + 2 * half
            here = jnp.logical_and(needed == residue, p == piece)

            @pl.when(here)
            def _():
                screen_local().wait()

            @pl.when(jnp.logical_not(here))
            def _():
                remote(screen_ref, screen.at[p], sw.at[0], rw.at[p], lax.rem(a + 1, ROWS), b).wait_recv()

            forward_copy(p).start()

    def forwarded(slot):
        for half in range(2):
            p = slot * 4 + 1 - core + 2 * half
            forward_copy(p).wait_recv()

    @pl.loop(0, 8)
    def _(i):
        row = lax.broadcasted_iota(jnp.int32, (128, PAIRS), 0) + i * 128
        col = lax.broadcasted_iota(jnp.int32, (128, PAIRS), 1)
        hit = jnp.logical_and((row & 31) == (col >> 5), (row >> 5) == (col & 31))
        swap[pl.ds(pl.multiple_of(i * 128, 128), 128)] = jnp.where(hit, 1.0, 0.0).astype(jnp.bfloat16)

    point = place[point_value]
    lane = lax.broadcasted_iota(jnp.int32, (8, QUART), 1)
    upper = jnp.zeros((8, QUART), jnp.float32)
    lower = jnp.zeros((8, QUART), jnp.float32)
    for c in range(NC):
        upper = jnp.where((lane & 31) == c, energy[point, NV + c], upper)
    for v in range(8):
        lower = jnp.where((lane >> 5) == v, energy[point, 8 * quarter + v], lower)
    gap[...] = upper - lower

    @pl.loop(0, COLS - 1)
    def _(d):
        second_copy(d).wait()

    @pl.loop(0, 6)
    def _(slot):
        for source in range(COLS):
            wide[source * 16 : source * 16 + 16] = landed[source, slot].astype(jnp.float32)
        for lanes in range(4):
            orb[slot, :, lanes * 128 : lanes * 128 + 128] = wide[pl.ds(lanes, 64, stride=4), :]

    def vec_second_copy(d):
        index = lax.rem(me + 4 * (d + 1), COLS)
        row, col = peer(index)
        return remote(vec_sent.at[d], vec_row.at[group], svb.at[d], rvb.at[d], row, col)

    def turn_copy(step, source):
        row, col = device(7 - beta, alpha, core)
        return remote(source, passed.at[step], st.at[step], rt.at[step], row, col)

    turned_order = order_of(7 - alpha)
    part_index = (turned_order // 4) * 4 + 2 * lax.rem(turned_order, 2) + core
    spread_core = lax.rem(turned_order // 2, 2)

    def spread_target(i):
        return device(lax.rem(alpha + i, 8), beta, spread_core)

    def spread_self(i):
        return jnp.logical_and(i == 0, spread_core == core)

    def spread_copy(step, i):
        row, col = spread_target(i)
        return remote(
            passed.at[step],
            column.at[step, part_index],
            sg.at[step, i],
            rg.at[step, part_index],
            row,
            col,
        )

    def spread_local(step, p):
        return pltpu.make_async_copy(passed.at[step], column.at[step, p], lg.at[step])

    def spread_start(step, source):
        turn_copy(step, source).wait()

        @pl.loop(0, ROWS)
        def _(i):
            @pl.when(spread_self(i))
            def _():
                spread_local(step, part_index).start()

            @pl.when(jnp.logical_not(spread_self(i)))
            def _():
                spread_copy(step, i).start()

    def spread_wait(step):
        @pl.loop(0, 8)
        def _(p):
            here = jnp.logical_and(spread_core == core, p == part_index)

            @pl.when(here)
            def _():
                spread_local(step, p).wait()

            @pl.when(jnp.logical_not(here))
            def _():
                remote(
                    passed.at[step],
                    column.at[step, p],
                    sg.at[step, 0],
                    rg.at[step, p],
                    lax.rem(a + 1, ROWS),
                    b,
                ).wait_recv()

    wrap = jnp.where(alpha >= beta, 0, 1)
    lane = lax.broadcasted_iota(jnp.int32, (32, 128), 1)
    low = lane < 64
    even = (lane & 32) == 0

    def build(slot, m, t):
        left, right = m, 4 + t
        for v in range(NV):
            valence[v * 32 : v * 32 + 32] = (orb[left, v : v + 1] * orb[right, :NV]).astype(jnp.bfloat16)
            conduct[v * 32 : v * 32 + 32] = (orb[right, NV + v : NV + v + 1] * orb[left, NV:]).astype(
                jnp.bfloat16
            )
        block = screen[pl.ds(slot * 4, 4)].reshape(NG, NG)
        amplitude[...] = jnp.dot(valence[...], block, preferred_element_type=jnp.float32).astype(jnp.bfloat16)
        for block in range(4):
            product[...] = lax.dot_general(
                amplitude[...],
                conduct[block * 256 : block * 256 + 256],
                (((1,), (1,)), ((), ())),
                preferred_element_type=jnp.float32,
            )
            for octet in range(8):
                for half in range(2):
                    s = [
                        product[octet * 128 + i * 32 : octet * 128 + i * 32 + 32, half * 128 : half * 128 + 128]
                        for i in range(4)
                    ]
                    u0 = jnp.where(low, s[0], pltpu.roll(s[2], 64, 1))
                    u2 = jnp.where(low, pltpu.roll(s[0], 64, 1), s[2])
                    u1 = jnp.where(low, s[1], pltpu.roll(s[3], 64, 1))
                    u3 = jnp.where(low, pltpu.roll(s[1], 64, 1), s[3])
                    turned = [
                        jnp.where(even, u0, pltpu.roll(u1, 32, 1)),
                        jnp.where(even, pltpu.roll(u0, 96, 1), u1),
                        jnp.where(even, u2, pltpu.roll(u3, 32, 1)),
                        jnp.where(even, pltpu.roll(u2, 96, 1), u3),
                    ]
                    first = block * 256 + half * 128
                    lanes = (octet % 2) * 128
                    for i in range(4):
                        tiles[m, octet // 2, t, first + i * 32 : first + i * 32 + 32, lanes : lanes + 128] = turned[
                            i
                        ].astype(jnp.bfloat16)

    arrive(level)

    @pl.loop(0, 4)
    def _(phase):
        slot = lax.rem(level + phase, 4)

        @pl.when(phase < 3)
        def _():
            arrive(lax.rem(slot + 1, 4))

        forwarded(slot)

        @pl.loop(0, 2)
        def _(t):
            build(slot, lax.rem(slot + wrap + core + 2 * t, 4), t)

        @pl.when(phase == 0)
        def _():
            vec_start()

        @pl.when(phase == 1)
        def _():
            @pl.loop(0, 8)
            def _(i):
                here = jnp.logical_and(vec_self, i == alpha)

                @pl.when(jnp.logical_not(here))
                def _():
                    vec_first_copy(i).wait_send()

            @pl.loop(0, 8)
            def _(i):
                here = jnp.logical_and(vec_self, i == a)

                @pl.when(here)
                def _():
                    vec_first_local().wait()

                @pl.when(jnp.logical_not(here))
                def _():
                    remote(
                        vec_ref, vec_got.at[i], sva.at[0], rva.at[i], lax.rem(a + 1, ROWS), b
                    ).wait_recv()

            for d in range(3):
                home = alpha + 8 * lax.rem(group + d + 1, 4)
                vec_sent[d] = vec_got[place[home] // 4]
                vec_second_copy(d).start()
            vec_row[group] = vec_got[place[point_value] // 4]

        @pl.when(phase == 2)
        def _():
            for d in range(3):
                vec_second_copy(d).wait()
            own[...] = vec_row[lax.rem(place[point_value], 4)]
            turn_copy(0, own).start()

    spread_start(0, own)

    @pl.loop(0, 8)
    def _(i):
        @pl.when(jnp.logical_not(screen_self(i)))
        def _():
            screen_copy(i).wait_send()

    for slot in range(4):
        for half in range(2):
            forward_copy(slot * 4 + core + 2 * half).wait_send()

    mine = own[...].astype(jnp.float32)
    levels = gap[0:1]

    def partial_copy(step, index):
        row, col = peer(index)
        return remote(sent.at[step, index], got.at[step, me], sp.at[step, index], rp.at[step, me], row, col)

    def partial_arrival(step, index):
        row, col = peer(index)
        return remote(sent.at[step, index], got.at[step, index], sp.at[step, index], rp.at[step, index], row, col)

    for step in range(3):
        spread_wait(step)
        for t in range(2):
            turned = jnp.zeros((NX, PAIRS), jnp.float32)
            for j in range(4):
                turned += jnp.dot(
                    column[step, t * 4 + j],
                    swap[j * QUART : j * QUART + QUART],
                    preferred_element_type=jnp.float32,
                )
            ordered[:, t * PAIRS : t * PAIRS + PAIRS] = turned.astype(jnp.bfloat16)

        @pl.loop(0, 4)
        def _(i):
            m = lax.rem(group + 1 + i, 4)
            for j in range(4):
                index = 4 * m + j
                sent[step, index] = jnp.dot(
                    ordered[...],
                    tiles[m, j].reshape(2 * PAIRS, QUART),
                    preferred_element_type=jnp.float32,
                ).astype(jnp.bfloat16)

                @pl.when(index != me)
                def _():
                    partial_copy(step, index).start()

        got[step, me] = sent[step, me]

        @pl.loop(0, COLS - 1)
        def _(d):
            partial_arrival(step, lax.rem(me + d + 1, COLS)).wait_recv()

        total = jnp.zeros((NX, QUART), jnp.float32)
        for source in range(COLS):
            total += got[step, source].astype(jnp.float32)
        if step == 0:
            new = (levels * mine + total) / SPREAD
            state[0] = new
        elif step == 1:
            new = 2.0 * ((levels * state[0] + total) / SPREAD) - mine
            state[1] = new
        else:
            new = 2.0 * ((levels * state[1] + total) / SPREAD) - state[0]
        if step < 2:
            rounded[step] = new.astype(jnp.bfloat16)
            turn_copy(step + 1, rounded.at[step]).start()
            spread_start(step + 1, rounded.at[step])
        else:
            final_row[group] = new.astype(jnp.bfloat16)

    def row_copy(d):
        row, col = peer(lax.rem(me + 4 * (d + 1), COLS))
        return remote(final_row.at[group], final_row.at[group], sa.at[d], ra.at[d], row, col)

    for d in range(3):
        row_copy(d).start()

    for step in range(3):

        @pl.loop(0, ROWS)
        def _(i):
            @pl.when(jnp.logical_not(spread_self(i)))
            def _():
                spread_copy(step, i).wait_send()

        @pl.loop(0, COLS - 1)
        def _(d):
            partial_copy(step, lax.rem(me + d + 1, COLS)).wait_send()

    for d in range(3):
        row_copy(d).wait()

    def last_copy(i):
        row = lax.rem(a + i, ROWS)
        return remote(final_sent.at[i], final_got.at[alpha], sb.at[i], rb.at[alpha], row, me)

    def last_self(i):
        return jnp.logical_and(i == 0, me == b)

    for i in range(ROWS):
        final_sent[i] = final_row[value[4 * lax.rem(a + i, ROWS) + group] // 8]

        @pl.when(jnp.logical_not(last_self(i)))
        def _():
            last_copy(i).start()

        @pl.when(last_self(i))
        def _():
            pltpu.make_async_copy(final_sent.at[i], final_got.at[alpha], lb).start()

    @pl.loop(0, 8)
    def _(label):
        here = jnp.logical_and(me == b, label == alpha)

        @pl.when(here)
        def _():
            pltpu.make_async_copy(final_sent.at[0], final_got.at[label], lb).wait()

        @pl.when(jnp.logical_not(here))
        def _():
            remote(
                final_sent.at[0], final_got.at[label], sb.at[0], rb.at[label], lax.rem(a + 1, ROWS), b
            ).wait_recv()

    out_ref[...] = final_got[lax.rem(value[4 * a + b // 4], 8)].astype(jnp.float32)

    @pl.loop(0, ROWS)
    def _(i):
        @pl.when(jnp.logical_not(last_self(i)))
        def _():
            last_copy(i).wait_send()


def per_device(orbitals, screened, kpoints, vectors, energies):
    dma = pltpu.SemaphoreType.DMA
    vmem = pl.BlockSpec(memory_space=pltpu.VMEM)
    smem = pl.BlockSpec(memory_space=pltpu.SMEM)
    anywhere = pl.BlockSpec(memory_space=pl.ANY)
    half, full = jnp.bfloat16, jnp.float32
    return pl.pallas_call(
        kernel,
        out_shape=jax.ShapeDtypeStruct((NX, QUART), full),
        in_specs=[smem, smem, vmem, anywhere, anywhere],
        out_specs=vmem,
        scratch_shapes=[
            pltpu.SMEM((NK,), jnp.int32),
            pltpu.VMEM((256, 128), full),
            pltpu.VMEM((4, 16, 128), half),
            pltpu.VMEM((NK, 16, 128), half),
            pltpu.VMEM((COLS, 6, 16, 128), half),
            pltpu.VMEM((COLS, 6, 16, 128), half),
            pltpu.VMEM((6, 64, NG), full),
            pltpu.VMEM((16, 128, NG), half),
            pltpu.VMEM((PAIRS, NG), half),
            pltpu.VMEM((PAIRS, NG), half),
            pltpu.VMEM((PAIRS, NG), half),
            pltpu.VMEM((PAIRS, 256), full),
            pltpu.VMEM((4, 4, 2, PAIRS, QUART), half),
            pltpu.VMEM((PAIRS, PAIRS), half),
            pltpu.VMEM((4, NX, QUART), half),
            pltpu.VMEM((7, NX, QUART), half),
            pltpu.VMEM((8, NX, QUART), half),
            pltpu.VMEM((NX, QUART), half),
            pltpu.VMEM((8, QUART), full),
            pltpu.VMEM((3, NX, QUART), half),
            pltpu.VMEM((3, 8, NX, QUART), half),
            pltpu.VMEM((NX, 2 * PAIRS), half),
            pltpu.VMEM((3, COLS, NX, QUART), half),
            pltpu.VMEM((3, COLS, NX, QUART), half),
            pltpu.VMEM((2, NX, QUART), half),
            pltpu.VMEM((2, NX, QUART), full),
            pltpu.VMEM((4, NX, QUART), half),
            pltpu.VMEM((8, NX, QUART), half),
            pltpu.VMEM((8, NX, QUART), half),
            dma((7,)),
            dma((7,)),
            dma((15,)),
            dma((15,)),
            dma((8,)),
            dma((16,)),
            dma,
            dma((16,)),
            dma((8,)),
            dma((8,)),
            dma,
            dma((3,)),
            dma((3,)),
            dma((3,)),
            dma((3,)),
            dma((3, 8)),
            dma((3, 8)),
            dma((3,)),
            dma((3, 16)),
            dma((3, 16)),
            dma((3,)),
            dma((3,)),
            dma((8,)),
            dma((8,)),
            dma,
        ],
        compiler_params=pltpu.CompilerParams(
            has_side_effects=True, collective_id=0, vmem_limit_bytes=56 << 20),
        name="mega",
    )(kpoints, energies, orbitals, screened, vectors)


def solution(mesh):
    placed = (P("row", "col", None), P(("row", "col"), None), P(), P(None, ("row", "col")), P())
    return jax.shard_map(
        per_device, mesh=mesh, in_specs=placed, out_specs=P(None, ("row", "col")), check_vma=False
    )
```

```python
import jax
import jax.numpy as jnp
from jax import lax
from jax.experimental import pallas as pl
from jax.experimental.pallas import tpu as pltpu
from jax.sharding import PartitionSpec as P

NV = 32
NC = 32
NG = 512
NX = 64
NK = 32
PAIRS = NV * NC
ROWS = 8
COLS = 16
SPREAD = 4.0
QUART = PAIRS // 4


def remote(src, dst, send_sem, recv_sem, row, col):
    return pltpu.make_async_remote_copy(
        src_ref=src,
        dst_ref=dst,
        send_sem=send_sem,
        recv_sem=recv_sem,
        device_id=(row, col),
        device_id_type=pl.DeviceIdType.MESH,
    )


def kernel(
    value,
    energy,
    orb_ref,
    screen_ref,
    vec_ref,
    out_ref,
    place,
    wide,
    orb_mine,
    orb_all,
    staged,
    landed,
    orb,
    screen,
    valence,
    conduct,
    amplitude,
    product,
    tiles,
    swap,
    vec_row,
    vec_sent,
    vec_got,
    own,
    gap,
    column,
    ordered,
    sent,
    got,
    rounded,
    state,
    final_row,
    final_sent,
    final_got,
    s1,
    r1,
    s2,
    r2,
    sw,
    rw,
    lw,
    sf,
    sva,
    rva,
    lva,
    svb,
    rvb,
    sg,
    rg,
    lg,
    sp,
    rp,
    sa,
    ra,
    sb,
    rb,
    lb,
):
    a = lax.axis_index("row")
    b = lax.axis_index("col")
    core = lax.rem(b, 2)
    alpha = b // 2
    level = a // 2
    side = lax.rem(a, 2)
    residue = 4 * side + b // 4
    piece = level * 4 + lax.rem(b, 4)
    needed = lax.rem(alpha - a + 8, 8)
    quarter = 2 * side + core
    point_value = alpha + 8 * level
    me = 2 * a + core
    plane_self = lax.rem(alpha, 2) == side
    spread_core = lax.rem(level, 2)
    spread_own = jnp.logical_and(alpha == a, spread_core == core)

    def plane_device(i):
        return 2 * level + i // 4, 4 * lax.rem(i, 4) + quarter

    def plane_owner(label):
        return 2 * level + lax.rem(alpha, 2), 2 * label + core

    barrier = pltpu.get_barrier_semaphore()

    def greet(row, col):
        pl.semaphore_signal(barrier, inc=1, device_id=(row, col), device_id_type=pl.DeviceIdType.MESH)

    def greet_other(row, col):
        @pl.when(jnp.logical_or(row != a, col != b))
        def _():
            greet(row, col)

    @pl.loop(0, ROWS - 1)
    def _(d):
        greet(lax.rem(a + d + 1, ROWS), b)
        greet(lax.rem(a + d + 1, ROWS), b + 1 - 2 * core)

    @pl.loop(0, COLS - 1)
    def _(d):
        greet(a, lax.rem(b + d + 1, COLS))

    @pl.loop(0, 8)
    def _(i):
        greet_other(2 * (i // 2) + needed // 4, 4 * lax.rem(needed, 4) + core + 2 * lax.rem(i, 2))
        greet_other(*plane_device(i))
        greet_other(*plane_owner(i))
        greet_other(4 * (i // 4) + 2 * core + lax.rem(i // 2, 2), 2 * a + lax.rem(i, 2))

    peers = 2 * (ROWS - 1) + COLS - 1 + 32
    peers -= jnp.where(needed == residue, 1, 0)
    peers -= jnp.where(plane_self, 2, 0)
    peers -= jnp.where(spread_own, 1, 0)
    pl.semaphore_wait(barrier, peers)

    for k in range(4):
        for lanes in range(4):
            wide[pl.ds(k * 16 + lanes, 4, stride=4), :] = orb_ref[k, :, lanes * 128 : lanes * 128 + 128].astype(
                jnp.float32
            )
    for k in range(4):
        orb_mine[k] = wide[k * 16 : k * 16 + 16].astype(jnp.bfloat16)

    def first_copy(d):
        return remote(
            orb_mine, orb_all.at[pl.ds(4 * a, 4)], s1.at[d], r1.at[d], lax.rem(a + d + 1, ROWS), b
        )

    @pl.loop(0, ROWS - 1)
    def _(d):
        first_copy(d).start()

    orb_all[pl.ds(4 * a, 4)] = orb_mine[...]

    def vec_first_copy(label):
        row, col = plane_owner(label)
        slot = 4 * side + b // 4
        return remote(vec_ref, vec_got.at[slot], sva.at[label], rva.at[slot], row, col)

    def vec_first_local():
        return pltpu.make_async_copy(vec_ref, vec_got.at[4 * side + b // 4], lva)

    def screen_target(label):
        return lax.rem(label - residue + 8, 8), 2 * label + core

    def screen_copy(i):
        row, col = screen_target(i)
        return remote(screen_ref, screen.at[piece], sw.at[i], rw.at[piece], row, col)

    def screen_local():
        return pltpu.make_async_copy(screen_ref, screen.at[piece], lw)

    def screen_self(i):
        row, col = screen_target(i)
        return jnp.logical_and(row == a, col == b)

    def forward_copy(p):
        return remote(screen.at[p], screen.at[p], sf.at[p], rw.at[p], a, b + 1 - 2 * core)

    @pl.loop(0, 32)
    def _(i):
        label = lax.rem(i + alpha, 8)
        turn = lax.rem(level - screen_target(label)[0] // 2 + 4, 4) == i // 8

        @pl.when(jnp.logical_and(turn, screen_self(label)))
        def _():
            screen_local().start()

        @pl.when(jnp.logical_and(turn, jnp.logical_not(screen_self(label))))
        def _():
            screen_copy(label).start()

    @pl.loop(0, NK)
    def _(wanted):
        found = jnp.int32(0)
        for k in range(NK):
            found = jnp.where(value[k] == wanted, k, found)
        place[wanted] = found

    @pl.loop(0, ROWS - 1)
    def _(d):
        first_copy(d).wait()

    @pl.loop(0, COLS)
    def _(dest):
        for m in range(4):
            staged[dest, m] = orb_all[place[dest // 2 + 8 * m]]
        for t in range(2):
            staged[dest, 4 + t] = orb_all[place[a + 8 * lax.rem(dest, 2) + 16 * t]]

    def second_copy(d):
        col = lax.rem(b + d + 1, COLS)
        return remote(staged.at[col], landed.at[b], s2.at[d], r2.at[d], a, col)

    @pl.loop(0, COLS - 1)
    def _(d):
        second_copy(d).start()

    landed[b] = staged[b]

    def vec_start():
        @pl.loop(0, 8)
        def _(i):
            label = lax.rem(i + alpha, 8)
            here = jnp.logical_and(plane_self, label == alpha)

            @pl.when(here)
            def _():
                vec_first_local().start()

            @pl.when(jnp.logical_not(here))
            def _():
                vec_first_copy(label).start()

    def arrive(slot):
        for half in range(2):
            p = slot * 4 + core + 2 * half
            here = jnp.logical_and(needed == residue, p == piece)

            @pl.when(here)
            def _():
                screen_local().wait()

            @pl.when(jnp.logical_not(here))
            def _():
                remote(screen_ref, screen.at[p], sw.at[0], rw.at[p], lax.rem(a + 1, ROWS), b).wait_recv()

            forward_copy(p).start()

    def forwarded(slot):
        for half in range(2):
            p = slot * 4 + 1 - core + 2 * half
            forward_copy(p).wait_recv()

    @pl.loop(0, 8)
    def _(i):
        row = lax.broadcasted_iota(jnp.int32, (128, PAIRS), 0) + i * 128
        col = lax.broadcasted_iota(jnp.int32, (128, PAIRS), 1)
        hit = jnp.logical_and((row & 31) == (col >> 5), (row >> 5) == (col & 31))
        swap[pl.ds(pl.multiple_of(i * 128, 128), 128)] = jnp.where(hit, 1.0, 0.0).astype(jnp.bfloat16)

    point = place[point_value]
    lane = lax.broadcasted_iota(jnp.int32, (8, QUART), 1)
    upper = jnp.zeros((8, QUART), jnp.float32)
    lower = jnp.zeros((8, QUART), jnp.float32)
    for c in range(NC):
        upper = jnp.where((lane & 31) == c, energy[point, NV + c], upper)
    for v in range(8):
        lower = jnp.where((lane >> 5) == v, energy[point, 8 * quarter + v], lower)
    gap[...] = upper - lower

    @pl.loop(0, COLS - 1)
    def _(d):
        second_copy(d).wait()

    @pl.loop(0, 6)
    def _(slot):
        for source in range(COLS):
            wide[source * 16 : source * 16 + 16] = landed[source, slot].astype(jnp.float32)
        for lanes in range(4):
            orb[slot, :, lanes * 128 : lanes * 128 + 128] = wide[pl.ds(lanes, 64, stride=4), :]

    def vec_second_copy(d):
        row = lax.rem(a + 2 * (d + 1), ROWS)
        return remote(vec_sent.at[d], vec_row.at[level], svb.at[d], rvb.at[d], row, b)

    part_index = (a // 4) * 4 + quarter

    def spread_copy(step, source, i):
        return remote(
            source,
            column.at[step, part_index],
            sg.at[step, i],
            rg.at[step, part_index],
            alpha,
            2 * lax.rem(alpha + i, 8) + spread_core,
        )

    def spread_local(step, source, p):
        return pltpu.make_async_copy(source, column.at[step, p], lg.at[step])

    def spread_self(i):
        return jnp.logical_and(i == 0, spread_own)

    def spread_start(step, source):
        @pl.loop(0, ROWS)
        def _(i):
            @pl.when(spread_self(i))
            def _():
                spread_local(step, source, part_index).start()

            @pl.when(jnp.logical_not(spread_self(i)))
            def _():
                spread_copy(step, source, i).start()

    def spread_wait(step, source):
        @pl.loop(0, 8)
        def _(p):
            here = jnp.logical_and(spread_own, p == part_index)

            @pl.when(here)
            def _():
                spread_local(step, source, p).wait()

            @pl.when(jnp.logical_not(here))
            def _():
                remote(
                    source,
                    column.at[step, p],
                    sg.at[step, 0],
                    rg.at[step, p],
                    lax.rem(a + 1, ROWS),
                    b,
                ).wait_recv()

    wrap = jnp.where(alpha >= a, 0, 1)
    lane = lax.broadcasted_iota(jnp.int32, (32, 128), 1)
    low = lane < 64
    even = (lane & 32) == 0

    def build(slot, m, t):
        left, right = m, 4 + t
        for v in range(NV):
            valence[v * 32 : v * 32 + 32] = (orb[left, v : v + 1] * orb[right, :NV]).astype(jnp.bfloat16)
            conduct[v * 32 : v * 32 + 32] = (orb[right, NV + v : NV + v + 1] * orb[left, NV:]).astype(
                jnp.bfloat16
            )
        block = screen[pl.ds(slot * 4, 4)].reshape(NG, NG)
        amplitude[...] = jnp.dot(valence[...], block, preferred_element_type=jnp.float32).astype(jnp.bfloat16)
        for block in range(4):
            product[...] = lax.dot_general(
                amplitude[...],
                conduct[block * 256 : block * 256 + 256],
                (((1,), (1,)), ((), ())),
                preferred_element_type=jnp.float32,
            )
            for octet in range(8):
                for half in range(2):
                    s = [
                        product[octet * 128 + i * 32 : octet * 128 + i * 32 + 32, half * 128 : half * 128 + 128]
                        for i in range(4)
                    ]
                    u0 = jnp.where(low, s[0], pltpu.roll(s[2], 64, 1))
                    u2 = jnp.where(low, pltpu.roll(s[0], 64, 1), s[2])
                    u1 = jnp.where(low, s[1], pltpu.roll(s[3], 64, 1))
                    u3 = jnp.where(low, pltpu.roll(s[1], 64, 1), s[3])
                    turned = [
                        jnp.where(even, u0, pltpu.roll(u1, 32, 1)),
                        jnp.where(even, pltpu.roll(u0, 96, 1), u1),
                        jnp.where(even, u2, pltpu.roll(u3, 32, 1)),
                        jnp.where(even, pltpu.roll(u2, 96, 1), u3),
                    ]
                    first = block * 256 + half * 128
                    lanes = (octet % 2) * 128
                    for i in range(4):
                        tiles[m, octet // 2, t, first + i * 32 : first + i * 32 + 32, lanes : lanes + 128] = turned[
                            i
                        ].astype(jnp.bfloat16)

    arrive(level)

    @pl.loop(0, 4)
    def _(phase):
        slot = lax.rem(level + phase, 4)

        @pl.when(phase < 3)
        def _():
            arrive(lax.rem(slot + 1, 4))

        forwarded(slot)

        @pl.loop(0, 2)
        def _(t):
            build(slot, lax.rem(slot + wrap + core + 2 * t, 4), t)

        @pl.when(phase == 0)
        def _():
            vec_start()

        @pl.when(phase == 1)
        def _():
            @pl.loop(0, 8)
            def _(i):
                here = jnp.logical_and(plane_self, i == alpha)

                @pl.when(jnp.logical_not(here))
                def _():
                    vec_first_copy(i).wait_send()

            @pl.loop(0, 8)
            def _(i):
                here = jnp.logical_and(plane_self, i == 4 * side + b // 4)

                @pl.when(here)
                def _():
                    vec_first_local().wait()

                @pl.when(jnp.logical_not(here))
                def _():
                    remote(
                        vec_ref, vec_got.at[i], sva.at[0], rva.at[i], lax.rem(a + 1, ROWS), b
                    ).wait_recv()

            for d in range(3):
                home = alpha + 8 * lax.rem(level + d + 1, 4)
                vec_sent[d] = vec_got[lax.rem(place[home], 8)]
                vec_second_copy(d).start()
            vec_row[level] = vec_got[lax.rem(place[point_value], 8)]

        @pl.when(phase == 2)
        def _():
            for d in range(3):
                vec_second_copy(d).wait()
            own[...] = vec_row[place[point_value] // 8]
            spread_start(0, own)

    @pl.loop(0, 8)
    def _(i):
        @pl.when(jnp.logical_not(screen_self(i)))
        def _():
            screen_copy(i).wait_send()

    for slot in range(4):
        for half in range(2):
            forward_copy(slot * 4 + core + 2 * half).wait_send()

    mine = own[...].astype(jnp.float32)
    levels = gap[0:1]

    def peer(index):
        return index // 2, 2 * alpha + lax.rem(index, 2)

    def partial_copy(step, index):
        row, col = peer(index)
        return remote(sent.at[step, index], got.at[step, me], sp.at[step, index], rp.at[step, me], row, col)

    def partial_arrival(step, index):
        row, col = peer(index)
        return remote(sent.at[step, index], got.at[step, index], sp.at[step, index], rp.at[step, index], row, col)

    for step in range(3):
        spread_wait(step, own if step == 0 else rounded.at[step - 1])
        for t in range(2):
            turned = jnp.zeros((NX, PAIRS), jnp.float32)
            for j in range(4):
                turned += jnp.dot(
                    column[step, t * 4 + j],
                    swap[j * QUART : j * QUART + QUART],
                    preferred_element_type=jnp.float32,
                )
            ordered[:, t * PAIRS : t * PAIRS + PAIRS] = turned.astype(jnp.bfloat16)

        @pl.loop(0, 4)
        def _(i):
            m = lax.rem(level + 1 + i, 4)
            for j in range(4):
                index = 4 * m + j
                sent[step, index] = jnp.dot(
                    ordered[...],
                    tiles[m, j].reshape(2 * PAIRS, QUART),
                    preferred_element_type=jnp.float32,
                ).astype(jnp.bfloat16)

                @pl.when(index != me)
                def _():
                    partial_copy(step, index).start()

        got[step, me] = sent[step, me]

        @pl.loop(0, COLS - 1)
        def _(d):
            partial_arrival(step, lax.rem(me + d + 1, COLS)).wait_recv()

        total = jnp.zeros((NX, QUART), jnp.float32)
        for source in range(COLS):
            total += got[step, source].astype(jnp.float32)
        if step == 0:
            new = (levels * mine + total) / SPREAD
            state[0] = new
        elif step == 1:
            new = 2.0 * ((levels * state[0] + total) / SPREAD) - mine
            state[1] = new
        else:
            new = 2.0 * ((levels * state[1] + total) / SPREAD) - state[0]
        if step < 2:
            rounded[step] = new.astype(jnp.bfloat16)
            spread_start(step + 1, rounded.at[step])
        else:
            final_row[level] = new.astype(jnp.bfloat16)

    def row_copy(d):
        row = lax.rem(a + 2 * (d + 1), ROWS)
        return remote(final_row.at[level], final_row.at[level], sa.at[d], ra.at[d], row, b)

    for d in range(3):
        row_copy(d).start()

    for step in range(3):

        @pl.loop(0, ROWS)
        def _(i):
            @pl.when(jnp.logical_not(spread_self(i)))
            def _():
                spread_copy(step, own if step == 0 else rounded.at[step - 1], i).wait_send()

        @pl.loop(0, COLS - 1)
        def _(d):
            partial_copy(step, lax.rem(me + d + 1, COLS)).wait_send()

    for d in range(3):
        row_copy(d).wait()

    def last_copy(i):
        row, col = plane_device(i)
        return remote(final_sent.at[i], final_got.at[alpha], sb.at[i], rb.at[alpha], row, col)

    def last_local(label):
        return pltpu.make_async_copy(final_sent.at[4 * side + b // 4], final_got.at[label], lb)

    def last_self(i):
        return jnp.logical_and(plane_self, i == 4 * side + b // 4)

    for i in range(ROWS):
        final_sent[i] = final_row[value[8 * level + i] // 8]

        @pl.when(jnp.logical_not(last_self(i)))
        def _():
            last_copy(i).start()

        @pl.when(last_self(i))
        def _():
            last_local(alpha).start()

    @pl.loop(0, 8)
    def _(label):
        here = jnp.logical_and(plane_self, label == alpha)

        @pl.when(here)
        def _():
            last_local(label).wait()

        @pl.when(jnp.logical_not(here))
        def _():
            remote(
                final_sent.at[0], final_got.at[label], sb.at[0], rb.at[label], lax.rem(a + 1, ROWS), b
            ).wait_recv()

    out_ref[...] = final_got[lax.rem(value[4 * a + b // 4], 8)].astype(jnp.float32)

    @pl.loop(0, ROWS)
    def _(i):
        @pl.when(jnp.logical_not(last_self(i)))
        def _():
            last_copy(i).wait_send()


def per_device(orbitals, screened, kpoints, vectors, energies):
    dma = pltpu.SemaphoreType.DMA
    vmem = pl.BlockSpec(memory_space=pltpu.VMEM)
    smem = pl.BlockSpec(memory_space=pltpu.SMEM)
    anywhere = pl.BlockSpec(memory_space=pl.ANY)
    half, full = jnp.bfloat16, jnp.float32
    return pl.pallas_call(
        kernel,
        out_shape=jax.ShapeDtypeStruct((NX, QUART), full),
        in_specs=[smem, smem, vmem, anywhere, anywhere],
        out_specs=vmem,
        scratch_shapes=[
            pltpu.SMEM((NK,), jnp.int32),
            pltpu.VMEM((256, 128), full),
            pltpu.VMEM((4, 16, 128), half),
            pltpu.VMEM((NK, 16, 128), half),
            pltpu.VMEM((COLS, 6, 16, 128), half),
            pltpu.VMEM((COLS, 6, 16, 128), half),
            pltpu.VMEM((6, 64, NG), full),
            pltpu.VMEM((16, 128, NG), half),
            pltpu.VMEM((PAIRS, NG), half),
            pltpu.VMEM((PAIRS, NG), half),
            pltpu.VMEM((PAIRS, NG), half),
            pltpu.VMEM((PAIRS, 256), full),
            pltpu.VMEM((4, 4, 2, PAIRS, QUART), half),
            pltpu.VMEM((PAIRS, PAIRS), half),
            pltpu.VMEM((4, NX, QUART), half),
            pltpu.VMEM((7, NX, QUART), half),
            pltpu.VMEM((8, NX, QUART), half),
            pltpu.VMEM((NX, QUART), half),
            pltpu.VMEM((8, QUART), full),
            pltpu.VMEM((3, 8, NX, QUART), half),
            pltpu.VMEM((NX, 2 * PAIRS), half),
            pltpu.VMEM((3, COLS, NX, QUART), half),
            pltpu.VMEM((3, COLS, NX, QUART), half),
            pltpu.VMEM((2, NX, QUART), half),
            pltpu.VMEM((2, NX, QUART), full),
            pltpu.VMEM((4, NX, QUART), half),
            pltpu.VMEM((8, NX, QUART), half),
            pltpu.VMEM((8, NX, QUART), half),
            dma((7,)),
            dma((7,)),
            dma((15,)),
            dma((15,)),
            dma((8,)),
            dma((16,)),
            dma,
            dma((16,)),
            dma((8,)),
            dma((8,)),
            dma,
            dma((3,)),
            dma((3,)),
            dma((3, 8)),
            dma((3, 8)),
            dma((3,)),
            dma((3, 16)),
            dma((3, 16)),
            dma((3,)),
            dma((3,)),
            dma((8,)),
            dma((8,)),
            dma,
        ],
        compiler_params=pltpu.CompilerParams(
            has_side_effects=True, collective_id=0, vmem_limit_bytes=56 << 20),
        name="mega",
    )(kpoints, energies, orbitals, screened, vectors)


def solution(mesh):
    placed = (P("row", "col", None), P(("row", "col"), None), P(), P(None, ("row", "col")), P())
    return jax.shard_map(
        per_device, mesh=mesh, in_specs=placed, out_specs=P(None, ("row", "col")), check_vma=False
    )
```

```python
import jax
import jax.numpy as jnp
from jax import lax
from jax.experimental import pallas as pl
from jax.experimental.pallas import tpu as pltpu
from jax.sharding import PartitionSpec as P

NV = 32
NC = 32
NG = 512
NX = 64
NK = 32
PAIRS = NV * NC
ROWS = 8
COLS = 16
SPREAD = 4.0
QUART = PAIRS // 4


def remote(src, dst, send_sem, recv_sem, row, col):
    return pltpu.make_async_remote_copy(
        src_ref=src,
        dst_ref=dst,
        send_sem=send_sem,
        recv_sem=recv_sem,
        device_id=(row, col),
        device_id_type=pl.DeviceIdType.MESH,
    )


def kernel(
    value,
    energy,
    orb_ref,
    screen_ref,
    vec_ref,
    out_ref,
    place,
    wide,
    orb_mine,
    orb_all,
    staged,
    landed,
    orb,
    screen,
    valence,
    conduct,
    amplitude,
    product,
    tiles,
    swap,
    vec_row,
    vec_sent,
    vec_got,
    own,
    own_swapped,
    gap,
    column,
    ordered,
    sent,
    got,
    rounded,
    state,
    final_row,
    final_sent,
    final_got,
    s1,
    r1,
    s2,
    r2,
    sw,
    rw,
    lw,
    sf,
    sva,
    rva,
    svb,
    rvb,
    sg,
    rg,
    sp,
    rp,
    sa,
    ra,
    sb,
    rb,
):
    a = lax.axis_index("row")
    b = lax.axis_index("col")
    core = lax.rem(b, 2)
    alpha = b // 2
    level = a // 2
    side = lax.rem(a, 2)
    residue = 4 * side + b // 4
    piece = level * 4 + lax.rem(b, 4)
    needed = lax.rem(alpha - a + 8, 8)
    quarter = 2 * side + core
    point_value = alpha + 8 * level
    me = 2 * a + core
    plane_self = lax.rem(alpha, 2) == side
    spread_core = lax.rem(level, 2)
    spread_own = jnp.logical_and(alpha == a, spread_core == core)

    def plane_device(i):
        return 2 * level + i // 4, 4 * lax.rem(i, 4) + quarter

    def plane_owner(label):
        return 2 * level + lax.rem(alpha, 2), 2 * label + core

    barrier = pltpu.get_barrier_semaphore()

    def greet(row, col):
        pl.semaphore_signal(barrier, inc=1, device_id=(row, col), device_id_type=pl.DeviceIdType.MESH)

    def greet_other(row, col):
        @pl.when(jnp.logical_or(row != a, col != b))
        def _():
            greet(row, col)

    @pl.loop(0, ROWS - 1)
    def _(d):
        greet(lax.rem(a + d + 1, ROWS), b)
        greet(lax.rem(a + d + 1, ROWS), b + 1 - 2 * core)

    @pl.loop(0, COLS - 1)
    def _(d):
        greet(a, lax.rem(b + d + 1, COLS))

    @pl.loop(0, 8)
    def _(i):
        greet_other(2 * (i // 2) + needed // 4, 4 * lax.rem(needed, 4) + core + 2 * lax.rem(i, 2))
        greet_other(*plane_device(i))
        greet_other(*plane_owner(i))
        greet_other(4 * (i // 4) + 2 * core + lax.rem(i // 2, 2), 2 * a + lax.rem(i, 2))

    peers = 2 * (ROWS - 1) + COLS - 1 + 32
    peers -= jnp.where(needed == residue, 1, 0)
    peers -= jnp.where(plane_self, 2, 0)
    peers -= jnp.where(spread_own, 1, 0)
    for k in range(4):
        for lanes in range(4):
            wide[pl.ds(k * 16 + lanes, 4, stride=4), :] = orb_ref[k, :, lanes * 128 : lanes * 128 + 128].astype(
                jnp.float32
            )
    for k in range(4):
        orb_mine[k] = wide[k * 16 : k * 16 + 16].astype(jnp.bfloat16)

    pl.semaphore_wait(barrier, peers)

    def first_copy(d):
        return remote(
            orb_mine, orb_all.at[pl.ds(4 * a, 4)], s1.at[0], r1.at[0], lax.rem(a + d + 1, ROWS), b
        )

    @pl.loop(0, ROWS - 1)
    def _(d):
        first_copy(d).start()

    orb_all[pl.ds(4 * a, 4)] = orb_mine[...]

    def vec_first_copy(label):
        row, col = plane_owner(label)
        slot = 4 * side + b // 4
        return remote(vec_ref, vec_got.at[slot], sva.at[0], rva.at[0], row, col)

    def vec_first_local():
        return pltpu.make_async_copy(vec_ref, vec_got.at[4 * side + b // 4], rva.at[0])

    def screen_target(label):
        return lax.rem(label - residue + 8, 8), 2 * label + core

    def screen_copy(i):
        row, col = screen_target(i)
        return remote(screen_ref, screen.at[piece], sw.at[i], rw.at[piece], row, col)

    def screen_local():
        return pltpu.make_async_copy(screen_ref, screen.at[piece], lw)

    def screen_self(i):
        row, col = screen_target(i)
        return jnp.logical_and(row == a, col == b)

    def forward_copy(p):
        return remote(screen.at[p], screen.at[p], sf.at[p], rw.at[p], a, b + 1 - 2 * core)

    def screen_start(i):
        label = lax.rem(i + alpha, 8)
        turn = lax.rem(level - screen_target(label)[0] // 2 + 4, 4) == i // 8

        @pl.when(jnp.logical_and(turn, screen_self(label)))
        def _():
            screen_local().start()

        @pl.when(jnp.logical_and(turn, jnp.logical_not(screen_self(label))))
        def _():
            screen_copy(label).start()

    @pl.loop(0, 16)
    def _(i):
        screen_start(i)

    @pl.loop(0, NK)
    def _(wanted):
        found = jnp.int32(0)
        for k in range(NK):
            found = jnp.where(value[k] == wanted, k, found)
        place[wanted] = found

    remote(orb_all.at[pl.ds(0, 28)], orb_all.at[pl.ds(0, 28)], s1.at[0], r1.at[0], lax.rem(a + 1, ROWS), b).wait()

    @pl.loop(0, COLS)
    def _(dest):
        for m in range(4):
            staged[dest, m] = orb_all[place[dest // 2 + 8 * m]]
        for t in range(2):
            staged[dest, 4 + t] = orb_all[place[a + 8 * lax.rem(dest, 2) + 16 * t]]

    def second_copy(d):
        col = lax.rem(b + d + 1, COLS)
        return remote(staged.at[col], landed.at[b], s2.at[0], r2.at[0], a, col)

    @pl.loop(0, COLS - 1)
    def _(d):
        second_copy(d).start()

    @pl.loop(16, 32)
    def _(i):
        screen_start(i)

    landed[b] = staged[b]

    def vec_start():
        @pl.loop(0, 8)
        def _(i):
            label = lax.rem(i + alpha, 8)
            here = jnp.logical_and(plane_self, label == alpha)

            @pl.when(here)
            def _():
                vec_first_local().start()

            @pl.when(jnp.logical_not(here))
            def _():
                vec_first_copy(label).start()

    def arrive(slot):
        for half in range(2):
            p = slot * 4 + core + 2 * half
            here = jnp.logical_and(needed == residue, p == piece)

            @pl.when(here)
            def _():
                screen_local().wait()

            @pl.when(jnp.logical_not(here))
            def _():
                remote(screen_ref, screen.at[p], sw.at[0], rw.at[p], lax.rem(a + 1, ROWS), b).wait_recv()

            forward_copy(p).start()

    def forwarded(slot):
        for half in range(2):
            p = slot * 4 + 1 - core + 2 * half
            forward_copy(p).wait_recv()

    row = lax.broadcasted_iota(jnp.int32, (QUART, QUART), 0)
    col = lax.broadcasted_iota(jnp.int32, (QUART, QUART), 1)
    hit = jnp.logical_and((row & 31) == (col >> 3), (row >> 5) == (col & 7))
    swap[...] = jnp.where(hit, 1.0, 0.0).astype(jnp.bfloat16)

    def swapped(block):
        return jnp.dot(block, swap[...], preferred_element_type=jnp.float32).astype(jnp.bfloat16)

    point = place[point_value]
    lane = lax.broadcasted_iota(jnp.int32, (8, QUART), 1)
    upper = jnp.zeros((8, QUART), jnp.float32)
    lower = jnp.zeros((8, QUART), jnp.float32)
    for c in range(NC):
        upper = jnp.where((lane & 31) == c, energy[point, NV + c], upper)
    for v in range(8):
        lower = jnp.where((lane >> 5) == v, energy[point, 8 * quarter + v], lower)
    gap[...] = upper - lower

    remote(
        staged.at[pl.ds(0, COLS - 1)], landed.at[pl.ds(0, COLS - 1)], s2.at[0], r2.at[0], a, lax.rem(b + 1, COLS)
    ).wait()

    @pl.loop(0, 6)
    def _(slot):
        for source in range(COLS):
            wide[source * 16 : source * 16 + 16] = landed[source, slot].astype(jnp.float32)
        for lanes in range(4):
            orb[slot, :, lanes * 128 : lanes * 128 + 128] = wide[pl.ds(lanes, 64, stride=4), :]

    def vec_second_copy(d):
        row = lax.rem(a + 2 * (d + 1), ROWS)
        return remote(vec_sent.at[d], vec_row.at[level], svb.at[d], rvb.at[d], row, b)

    part_index = (a // 4) * 4 + quarter

    def spread_copy(step, source, i):
        return remote(
            source,
            column.at[step, part_index],
            sg.at[step],
            rg.at[step],
            alpha,
            2 * lax.rem(alpha + i, 8) + spread_core,
        )

    def spread_local(step, source, p):
        return pltpu.make_async_copy(source, column.at[step, p], rg.at[step])

    def spread_self(i):
        return jnp.logical_and(i == 0, spread_own)

    def spread_start(step, source):
        @pl.loop(0, ROWS)
        def _(i):
            @pl.when(spread_self(i))
            def _():
                spread_local(step, source, part_index).start()

            @pl.when(jnp.logical_not(spread_self(i)))
            def _():
                spread_copy(step, source, i).start()

    def spread_all(step, count):
        return remote(
            column.at[step, pl.ds(0, count)],
            column.at[step, pl.ds(0, count)],
            sg.at[step],
            rg.at[step],
            lax.rem(a + 1, ROWS),
            b,
        )

    wrap = jnp.where(alpha >= a, 0, 1)
    lane = lax.broadcasted_iota(jnp.int32, (32, 128), 1)
    low = lane < 64
    even = (lane & 32) == 0

    def build(slot, m, t):
        left, right = m, 4 + t
        for v in range(NV):
            valence[v * 32 : v * 32 + 32] = (orb[left, v : v + 1] * orb[right, :NV]).astype(jnp.bfloat16)
            conduct[v * 32 : v * 32 + 32] = (orb[right, NV + v : NV + v + 1] * orb[left, NV:]).astype(
                jnp.bfloat16
            )
        block = screen[pl.ds(slot * 4, 4)].reshape(NG, NG)
        for chunk in range(4):
            rows = slice(chunk * 256, chunk * 256 + 256)
            amplitude[rows] = jnp.dot(valence[rows], block, preferred_element_type=jnp.float32).astype(
                jnp.bfloat16
            )

        def multiply(unit):
            block, chunk = divmod(unit, 4)
            product[unit % 2] = lax.dot_general(
                amplitude[chunk * 256 : chunk * 256 + 256],
                conduct[block * 256 : block * 256 + 256],
                (((1,), (1,)), ((), ())),
                preferred_element_type=jnp.float32,
            )

        def turn(unit):
            block, chunk = divmod(unit, 4)
            for octet in range(2):
                for half in range(2):
                    s = [
                        product[
                            unit % 2,
                            octet * 128 + i * 32 : octet * 128 + i * 32 + 32,
                            half * 128 : half * 128 + 128,
                        ]
                        for i in range(4)
                    ]
                    u0 = jnp.where(low, s[0], pltpu.roll(s[2], 64, 1))
                    u2 = jnp.where(low, pltpu.roll(s[0], 64, 1), s[2])
                    u1 = jnp.where(low, s[1], pltpu.roll(s[3], 64, 1))
                    u3 = jnp.where(low, pltpu.roll(s[1], 64, 1), s[3])
                    turned = [
                        jnp.where(even, u0, pltpu.roll(u1, 32, 1)),
                        jnp.where(even, pltpu.roll(u0, 96, 1), u1),
                        jnp.where(even, u2, pltpu.roll(u3, 32, 1)),
                        jnp.where(even, pltpu.roll(u2, 96, 1), u3),
                    ]
                    for j in range(4):
                        first = j * QUART + block * 64 + half * 32
                        tiles[m, chunk, t, first : first + 32, octet * 128 : octet * 128 + 128] = jnp.concatenate(
                            [turned[i][j * 8 : j * 8 + 8] for i in range(4)], axis=0
                        ).astype(jnp.bfloat16)

        multiply(0)
        for unit in range(1, 16):
            multiply(unit)
            turn(unit - 1)
        turn(15)

    arrive(level)

    @pl.loop(0, 4)
    def _(phase):
        slot = lax.rem(level + phase, 4)

        @pl.when(phase < 3)
        def _():
            arrive(lax.rem(slot + 1, 4))

        forwarded(slot)

        @pl.loop(0, 2)
        def _(t):
            build(slot, lax.rem(slot + wrap + core + 2 * t, 4), t)

        @pl.when(phase == 0)
        def _():
            vec_start()

        @pl.when(phase == 1)
        def _():
            def vec_all(count):
                return remote(
                    vec_got.at[pl.ds(0, count)],
                    vec_got.at[pl.ds(0, count)],
                    sva.at[0],
                    rva.at[0],
                    lax.rem(a + 1, ROWS),
                    b,
                )

            @pl.when(plane_self)
            def _():
                vec_all(7).wait_send()

            @pl.when(jnp.logical_not(plane_self))
            def _():
                vec_all(8).wait_send()

            vec_all(8).wait_recv()
            for d in range(3):
                home = alpha + 8 * lax.rem(level + d + 1, 4)
                vec_sent[d] = vec_got[lax.rem(place[home], 8)]
                vec_second_copy(d).start()
            vec_row[level] = vec_got[lax.rem(place[point_value], 8)]

        @pl.when(phase == 2)
        def _():
            for d in range(3):
                vec_second_copy(d).wait()
            own[...] = vec_row[place[point_value] // 8]
            own_swapped[...] = swapped(own[...])
            spread_start(0, own_swapped)

    @pl.loop(0, 8)
    def _(i):
        @pl.when(jnp.logical_not(screen_self(i)))
        def _():
            screen_copy(i).wait_send()

    for slot in range(4):
        for half in range(2):
            forward_copy(slot * 4 + core + 2 * half).wait_send()

    mine = own[...].astype(jnp.float32)
    levels = gap[0:1]

    def peer(index):
        return index // 2, 2 * alpha + lax.rem(index, 2)

    def partial_copy(step, index):
        row, col = peer(index)
        return remote(sent.at[step, index], got.at[step, me], sp.at[step], rp.at[step], row, col)

    def partial_all(step):
        return remote(
            sent.at[step, pl.ds(0, COLS - 1)],
            got.at[step, pl.ds(0, COLS - 1)],
            sp.at[step],
            rp.at[step],
            lax.rem(a + 1, ROWS),
            b,
        )

    for step in range(3):
        spread_all(step, 8).wait_recv()
        for p in range(8):
            ordered[:, p * QUART : p * QUART + QUART] = column[step, p]

        @pl.loop(0, 4)
        def _(i):
            m = lax.rem(level + 1 + i, 4)
            for j in range(4):
                sent[step, 4 * m + j] = jnp.dot(
                    ordered[...],
                    tiles[m, j].reshape(2 * PAIRS, QUART),
                    preferred_element_type=jnp.float32,
                ).astype(jnp.bfloat16)
            for j in range(4):

                @pl.when(4 * m + j != me)
                def _():
                    partial_copy(step, 4 * m + j).start()

        got[step, me] = sent[step, me]
        partial_all(step).wait_recv()
        total = jnp.zeros((NX, QUART), jnp.float32)
        for source in range(COLS):
            total += got[step, source].astype(jnp.float32)
        if step == 0:
            new = (levels * mine + total) / SPREAD
            state[0] = new
        elif step == 1:
            new = 2.0 * ((levels * state[0] + total) / SPREAD) - mine
            state[1] = new
        else:
            new = 2.0 * ((levels * state[1] + total) / SPREAD) - state[0]
        if step < 2:
            rounded[step] = swapped(new.astype(jnp.bfloat16))
            spread_start(step + 1, rounded.at[step])
        else:
            final_row[level] = new.astype(jnp.bfloat16)

    def row_copy(d):
        row = lax.rem(a + 2 * (d + 1), ROWS)
        return remote(final_row.at[level], final_row.at[level], sa.at[0], ra.at[0], row, b)

    for d in range(3):
        row_copy(d).start()

    for step in range(3):
        partial_all(step).wait_send()

        @pl.when(spread_own)
        def _():
            spread_all(step, 7).wait_send()

        @pl.when(jnp.logical_not(spread_own))
        def _():
            spread_all(step, 8).wait_send()

    remote(
        final_row.at[pl.ds(0, 3)], final_row.at[pl.ds(0, 3)], sa.at[0], ra.at[0], lax.rem(a + 1, ROWS), b
    ).wait()

    def last_copy(i):
        row, col = plane_device(i)
        return remote(final_sent.at[i], final_got.at[alpha], sb.at[0], rb.at[0], row, col)

    def last_local(label):
        return pltpu.make_async_copy(final_sent.at[4 * side + b // 4], final_got.at[label], rb.at[0])

    def last_self(i):
        return jnp.logical_and(plane_self, i == 4 * side + b // 4)

    for i in range(ROWS):
        final_sent[i] = final_row[value[8 * level + i] // 8]

        @pl.when(jnp.logical_not(last_self(i)))
        def _():
            last_copy(i).start()

        @pl.when(last_self(i))
        def _():
            last_local(alpha).start()

    def last_all(count):
        return remote(
            final_sent.at[pl.ds(0, count)],
            final_got.at[pl.ds(0, count)],
            sb.at[0],
            rb.at[0],
            lax.rem(a + 1, ROWS),
            b,
        )

    last_all(8).wait_recv()
    out_ref[...] = final_got[lax.rem(value[4 * a + b // 4], 8)].astype(jnp.float32)

    @pl.when(plane_self)
    def _():
        last_all(7).wait_send()

    @pl.when(jnp.logical_not(plane_self))
    def _():
        last_all(8).wait_send()


def per_device(orbitals, screened, kpoints, vectors, energies):
    dma = pltpu.SemaphoreType.DMA
    vmem = pl.BlockSpec(memory_space=pltpu.VMEM)
    smem = pl.BlockSpec(memory_space=pltpu.SMEM)
    anywhere = pl.BlockSpec(memory_space=pl.ANY)
    half, full = jnp.bfloat16, jnp.float32
    return pl.pallas_call(
        kernel,
        out_shape=jax.ShapeDtypeStruct((NX, QUART), full),
        in_specs=[smem, smem, vmem, anywhere, anywhere],
        out_specs=vmem,
        scratch_shapes=[
            pltpu.SMEM((NK,), jnp.int32),
            pltpu.VMEM((256, 128), full),
            pltpu.VMEM((4, 16, 128), half),
            pltpu.VMEM((NK, 16, 128), half),
            pltpu.VMEM((COLS, 6, 16, 128), half),
            pltpu.VMEM((COLS, 6, 16, 128), half),
            pltpu.VMEM((6, 64, NG), full),
            pltpu.VMEM((16, 128, NG), half),
            pltpu.VMEM((PAIRS, NG), half),
            pltpu.VMEM((PAIRS, NG), half),
            pltpu.VMEM((PAIRS, NG), half),
            pltpu.VMEM((2, 256, 256), full),
            pltpu.VMEM((4, 4, 2, PAIRS, QUART), half),
            pltpu.VMEM((QUART, QUART), half),
            pltpu.VMEM((4, NX, QUART), half),
            pltpu.VMEM((7, NX, QUART), half),
            pltpu.VMEM((8, NX, QUART), half),
            pltpu.VMEM((NX, QUART), half),
            pltpu.VMEM((NX, QUART), half),
            pltpu.VMEM((8, QUART), full),
            pltpu.VMEM((3, 8, NX, QUART), half),
            pltpu.VMEM((NX, 2 * PAIRS), half),
            pltpu.VMEM((3, COLS, NX, QUART), half),
            pltpu.VMEM((3, COLS, NX, QUART), half),
            pltpu.VMEM((2, NX, QUART), half),
            pltpu.VMEM((2, NX, QUART), full),
            pltpu.VMEM((4, NX, QUART), half),
            pltpu.VMEM((8, NX, QUART), half),
            pltpu.VMEM((8, NX, QUART), half),
            dma((1,)),
            dma((1,)),
            dma((1,)),
            dma((1,)),
            dma((8,)),
            dma((16,)),
            dma,
            dma((16,)),
            dma((1,)),
            dma((1,)),
            dma((3,)),
            dma((3,)),
            dma((3,)),
            dma((3,)),
            dma((3,)),
            dma((3,)),
            dma((1,)),
            dma((1,)),
            dma((1,)),
            dma((1,)),
        ],
        compiler_params=pltpu.CompilerParams(
            has_side_effects=True, collective_id=0, vmem_limit_bytes=56 << 20),
        name="mega",
    )(kpoints, energies, orbitals, screened, vectors)


def solution(mesh):
    placed = (P("row", "col", None), P(("row", "col"), None), P(), P(None, ("row", "col")), P())
    return jax.shard_map(
        per_device, mesh=mesh, in_specs=placed, out_specs=P(None, ("row", "col")), check_vma=False
    )
```

```python
import jax
import jax.numpy as jnp
from jax import lax
from jax.experimental import pallas as pl
from jax.experimental.pallas import tpu as pltpu
from jax.sharding import PartitionSpec as P

NV = 32
NC = 32
NG = 512
NX = 64
NK = 32
PAIRS = NV * NC
ROWS = 8
COLS = 16
SPREAD = 4.0
QUART = PAIRS // 4


def remote(src, dst, send_sem, recv_sem, row, col):
    return pltpu.make_async_remote_copy(
        src_ref=src,
        dst_ref=dst,
        send_sem=send_sem,
        recv_sem=recv_sem,
        device_id=(row, col),
        device_id_type=pl.DeviceIdType.MESH,
    )


def kernel(
    value,
    energy,
    orb_ref,
    screen_ref,
    vec_ref,
    out_ref,
    place,
    wide,
    orb_mine,
    orb_all,
    staged,
    landed,
    orb,
    screen,
    valence,
    conduct,
    amplitude,
    product,
    tiles,
    swap,
    vec_row,
    vec_sent,
    vec_got,
    own,
    own_swapped,
    gap,
    column,
    ordered,
    sent,
    got,
    pair_sent,
    pair_got,
    rounded,
    state,
    final_row,
    final_sent,
    final_got,
    s1,
    r1,
    s2,
    r2,
    sw,
    rw,
    lw,
    sf,
    sva,
    rva,
    svb,
    rvb,
    sg,
    rg,
    sp,
    rp,
    sa,
    ra,
    sb,
    rb,
    ss,
    rs,
):
    a = lax.axis_index("row")
    b = lax.axis_index("col")
    core = lax.rem(b, 2)
    alpha = b // 2
    level = a // 2
    side = lax.rem(a, 2)
    residue = 4 * side + b // 4
    piece = level * 4 + lax.rem(b, 4)
    needed = lax.rem(alpha - a + 8, 8)
    quarter = 2 * side + core
    point_value = alpha + 8 * level
    plane_self = lax.rem(alpha, 2) == side
    spread_core = lax.rem(level, 2)
    spread_own = jnp.logical_and(alpha == a, spread_core == core)

    def plane_device(i):
        return 2 * level + i // 4, 4 * lax.rem(i, 4) + quarter

    def plane_owner(label):
        return 2 * level + lax.rem(alpha, 2), 2 * label + core

    barrier = pltpu.get_barrier_semaphore()

    def greet(row, col):
        pl.semaphore_signal(barrier, inc=1, device_id=(row, col), device_id_type=pl.DeviceIdType.MESH)

    def greet_other(row, col):
        @pl.when(jnp.logical_or(row != a, col != b))
        def _():
            greet(row, col)

    @pl.loop(0, ROWS - 1)
    def _(d):
        greet(lax.rem(a + d + 1, ROWS), b)

    @pl.loop(0, COLS - 1)
    def _(d):
        greet(a, lax.rem(b + d + 1, COLS))

    @pl.loop(0, 8)
    def _(i):
        greet_other(2 * (i // 2) + needed // 4, 4 * lax.rem(needed, 4) + core + 2 * lax.rem(i, 2))
        greet_other(*plane_device(i))
        greet_other(*plane_owner(i))
        greet_other(4 * (i // 4) + 2 * core + lax.rem(i // 2, 2), 2 * a + lax.rem(i, 2))

    peers = ROWS - 1 + COLS - 1 + 32
    peers -= jnp.where(needed == residue, 1, 0)
    peers -= jnp.where(plane_self, 2, 0)
    peers -= jnp.where(spread_own, 1, 0)
    for k in range(4):
        for lanes in range(4):
            wide[pl.ds(k * 16 + lanes, 4, stride=4), :] = orb_ref[k, :, lanes * 128 : lanes * 128 + 128].astype(
                jnp.float32
            )
    for k in range(4):
        orb_mine[k] = wide[k * 16 : k * 16 + 16].astype(jnp.bfloat16)

    pl.semaphore_wait(barrier, peers)

    def first_copy(d):
        return remote(
            orb_mine, orb_all.at[pl.ds(4 * a, 4)], s1.at[0], r1.at[0], lax.rem(a + d + 1, ROWS), b
        )

    @pl.loop(0, ROWS - 1)
    def _(d):
        first_copy(d).start()

    orb_all[pl.ds(4 * a, 4)] = orb_mine[...]

    def vec_first_copy(label):
        row, col = plane_owner(label)
        slot = 4 * side + b // 4
        return remote(vec_ref, vec_got.at[slot], sva.at[0], rva.at[0], row, col)

    def vec_first_local():
        return pltpu.make_async_copy(vec_ref, vec_got.at[4 * side + b // 4], rva.at[0])

    def screen_target(label):
        return lax.rem(label - residue + 8, 8), 2 * label + core

    def screen_copy(i):
        row, col = screen_target(i)
        return remote(screen_ref, screen.at[piece], sw.at[i], rw.at[piece], row, col)

    def screen_local():
        return pltpu.make_async_copy(screen_ref, screen.at[piece], lw)

    def screen_self(i):
        row, col = screen_target(i)
        return jnp.logical_and(row == a, col == b)

    def forward_copy(p):
        return remote(screen.at[p], screen.at[p], sf.at[p], rw.at[p], a, b + 1 - 2 * core)

    def screen_start(i):
        label = lax.rem(i + alpha, 8)
        turn = lax.rem(level - screen_target(label)[0] // 2 + 4, 4) == i // 8

        @pl.when(jnp.logical_and(turn, screen_self(label)))
        def _():
            screen_local().start()

        @pl.when(jnp.logical_and(turn, jnp.logical_not(screen_self(label))))
        def _():
            screen_copy(label).start()

    @pl.loop(0, 8)
    def _(i):
        screen_start(i)

    @pl.loop(0, NK)
    def _(wanted):
        found = jnp.int32(0)
        for k in range(NK):
            found = jnp.where(value[k] == wanted, k, found)
        place[wanted] = found

    remote(orb_all.at[pl.ds(0, 28)], orb_all.at[pl.ds(0, 28)], s1.at[0], r1.at[0], lax.rem(a + 1, ROWS), b).wait()

    @pl.loop(0, COLS)
    def _(dest):
        for m in range(4):
            staged[dest, m] = orb_all[place[dest // 2 + 8 * m]]
        for t in range(2):
            staged[dest, 4 + t] = orb_all[place[a + 8 * lax.rem(dest, 2) + 16 * t]]

    def second_copy(d):
        col = lax.rem(b + d + 1, COLS)
        return remote(staged.at[col], landed.at[b], s2.at[0], r2.at[0], a, col)

    @pl.loop(0, COLS - 1)
    def _(d):
        second_copy(d).start()

    @pl.loop(8, 32)
    def _(i):
        screen_start(i)

    landed[b] = staged[b]

    def vec_start():
        @pl.loop(0, 8)
        def _(i):
            label = lax.rem(i + alpha, 8)
            here = jnp.logical_and(plane_self, label == alpha)

            @pl.when(here)
            def _():
                vec_first_local().start()

            @pl.when(jnp.logical_not(here))
            def _():
                vec_first_copy(label).start()

    def arrive(slot):
        for half in range(2):
            p = slot * 4 + core + 2 * half
            here = jnp.logical_and(needed == residue, p == piece)

            @pl.when(here)
            def _():
                screen_local().wait()

            @pl.when(jnp.logical_not(here))
            def _():
                remote(screen_ref, screen.at[p], sw.at[0], rw.at[p], lax.rem(a + 1, ROWS), b).wait_recv()

            forward_copy(p).start()

    def forwarded(slot):
        for half in range(2):
            p = slot * 4 + 1 - core + 2 * half
            forward_copy(p).wait_recv()

    row = lax.broadcasted_iota(jnp.int32, (QUART, QUART), 0)
    col = lax.broadcasted_iota(jnp.int32, (QUART, QUART), 1)
    hit = jnp.logical_and((row & 31) == (col >> 3), (row >> 5) == (col & 7))
    swap[...] = jnp.where(hit, 1.0, 0.0).astype(jnp.bfloat16)

    def swapped(block):
        return jnp.dot(block, swap[...], preferred_element_type=jnp.float32).astype(jnp.bfloat16)

    point = place[point_value]
    lane = lax.broadcasted_iota(jnp.int32, (8, QUART), 1)
    upper = jnp.zeros((8, QUART), jnp.float32)
    lower = jnp.zeros((8, QUART), jnp.float32)
    for c in range(NC):
        upper = jnp.where((lane & 31) == c, energy[point, NV + c], upper)
    for v in range(8):
        lower = jnp.where((lane >> 5) == v, energy[point, 8 * quarter + v], lower)
    gap[...] = upper - lower

    remote(
        staged.at[pl.ds(0, COLS - 1)], landed.at[pl.ds(0, COLS - 1)], s2.at[0], r2.at[0], a, lax.rem(b + 1, COLS)
    ).wait()

    @pl.loop(0, 6)
    def _(slot):
        for source in range(COLS):
            wide[source * 16 : source * 16 + 16] = landed[source, slot].astype(jnp.float32)
        for lanes in range(4):
            orb[slot, :, lanes * 128 : lanes * 128 + 128] = wide[pl.ds(lanes, 64, stride=4), :]

    def vec_second_copy(d):
        row = lax.rem(a + 2 * (d + 1), ROWS)
        return remote(vec_sent.at[d], vec_row.at[level], svb.at[d], rvb.at[d], row, b)

    part_index = (a // 4) * 4 + quarter

    def spread_copy(step, source, i):
        return remote(
            source,
            column.at[step, part_index],
            sg.at[step],
            rg.at[step],
            alpha,
            2 * lax.rem(alpha + i, 8) + spread_core,
        )

    def spread_local(step, source, p):
        return pltpu.make_async_copy(source, column.at[step, p], rg.at[step])

    def spread_self(i):
        return jnp.logical_and(i == 0, spread_own)

    def spread_start(step, source):
        @pl.loop(0, ROWS)
        def _(i):
            @pl.when(spread_self(i))
            def _():
                spread_local(step, source, part_index).start()

            @pl.when(jnp.logical_not(spread_self(i)))
            def _():
                spread_copy(step, source, i).start()

    def spread_all(step, count):
        return remote(
            column.at[step, pl.ds(0, count)],
            column.at[step, pl.ds(0, count)],
            sg.at[step],
            rg.at[step],
            lax.rem(a + 1, ROWS),
            b,
        )

    wrap = jnp.where(alpha >= a, 0, 1)
    lane = lax.broadcasted_iota(jnp.int32, (32, 128), 1)
    low = lane < 64
    even = (lane & 32) == 0

    def build(slot, m, t):
        left, right = m, 4 + t
        for v in range(NV):
            valence[v * 32 : v * 32 + 32] = (orb[left, v : v + 1] * orb[right, :NV]).astype(jnp.bfloat16)
            conduct[v * 32 : v * 32 + 32] = (orb[right, NV + v : NV + v + 1] * orb[left, NV:]).astype(
                jnp.bfloat16
            )
        block = screen[pl.ds(slot * 4, 4)].reshape(NG, NG)
        for chunk in range(4):
            rows = slice(chunk * 256, chunk * 256 + 256)
            amplitude[rows] = jnp.dot(valence[rows], block, preferred_element_type=jnp.float32).astype(
                jnp.bfloat16
            )

        def multiply(unit):
            block, chunk = divmod(unit, 4)
            product[unit % 2] = lax.dot_general(
                amplitude[chunk * 256 : chunk * 256 + 256],
                conduct[block * 256 : block * 256 + 256],
                (((1,), (1,)), ((), ())),
                preferred_element_type=jnp.float32,
            )

        def turn(unit):
            block, chunk = divmod(unit, 4)
            for octet in range(2):
                for half in range(2):
                    s = [
                        product[
                            unit % 2,
                            octet * 128 + i * 32 : octet * 128 + i * 32 + 32,
                            half * 128 : half * 128 + 128,
                        ]
                        for i in range(4)
                    ]
                    u0 = jnp.where(low, s[0], pltpu.roll(s[2], 64, 1))
                    u2 = jnp.where(low, pltpu.roll(s[0], 64, 1), s[2])
                    u1 = jnp.where(low, s[1], pltpu.roll(s[3], 64, 1))
                    u3 = jnp.where(low, pltpu.roll(s[1], 64, 1), s[3])
                    turned = [
                        jnp.where(even, u0, pltpu.roll(u1, 32, 1)),
                        jnp.where(even, pltpu.roll(u0, 96, 1), u1),
                        jnp.where(even, u2, pltpu.roll(u3, 32, 1)),
                        jnp.where(even, pltpu.roll(u2, 96, 1), u3),
                    ]
                    for j in range(4):
                        first = j * QUART + block * 64 + half * 32
                        tiles[m, chunk, t, first : first + 32, octet * 128 : octet * 128 + 128] = jnp.concatenate(
                            [turned[i][j * 8 : j * 8 + 8] for i in range(4)], axis=0
                        ).astype(jnp.bfloat16)

        multiply(0)
        for unit in range(1, 16):
            multiply(unit)
            turn(unit - 1)
        turn(15)

    arrive(level)

    @pl.loop(0, 4)
    def _(phase):
        slot = lax.rem(level + phase, 4)

        forwarded(slot)

        @pl.loop(0, 2)
        def _(t):
            @pl.when(jnp.logical_and(t == 1, phase < 3))
            def _():
                arrive(lax.rem(slot + 1, 4))

            build(slot, lax.rem(slot + wrap + core + 2 * t, 4), t)

        @pl.when(phase == 0)
        def _():
            vec_start()

        @pl.when(phase == 1)
        def _():
            def vec_all(count):
                return remote(
                    vec_got.at[pl.ds(0, count)],
                    vec_got.at[pl.ds(0, count)],
                    sva.at[0],
                    rva.at[0],
                    lax.rem(a + 1, ROWS),
                    b,
                )

            @pl.when(plane_self)
            def _():
                vec_all(7).wait_send()

            @pl.when(jnp.logical_not(plane_self))
            def _():
                vec_all(8).wait_send()

            vec_all(8).wait_recv()
            for d in range(3):
                home = alpha + 8 * lax.rem(level + d + 1, 4)
                vec_sent[d] = vec_got[lax.rem(place[home], 8)]
                vec_second_copy(d).start()
            vec_row[level] = vec_got[lax.rem(place[point_value], 8)]

        @pl.when(phase == 2)
        def _():
            for d in range(3):
                vec_second_copy(d).wait()
            own[...] = vec_row[place[point_value] // 8]
            own_swapped[...] = swapped(own[...])
            spread_start(0, own_swapped)

    @pl.loop(0, 8)
    def _(i):
        @pl.when(jnp.logical_not(screen_self(i)))
        def _():
            screen_copy(i).wait_send()

    for slot in range(4):
        for half in range(2):
            forward_copy(slot * 4 + core + 2 * half).wait_send()

    mine = own[...].astype(jnp.float32)
    levels = gap[0:1]

    def pair_copy(step, m):
        return remote(
            pair_sent.at[step, m],
            pair_got.at[step, m],
            ss.at[step, m],
            rs.at[step, m],
            a,
            b + 1 - 2 * core,
        )

    def partial_copy(step, row):
        return remote(sent.at[step, row], got.at[step, a], sp.at[step], rp.at[step], row, b)

    def partial_all(step):
        return remote(
            sent.at[step, pl.ds(0, ROWS - 1)],
            got.at[step, pl.ds(0, ROWS - 1)],
            sp.at[step],
            rp.at[step],
            lax.rem(a + 1, ROWS),
            b,
        )

    for step in range(3):
        spread_all(step, 8).wait_recv()
        for p in range(8):
            ordered[:, p * QUART : p * QUART + QUART] = column[step, p]

        @pl.loop(0, 4)
        def _(i):
            m = lax.rem(level + 1 + i, 4)
            for half in range(2):
                pair_sent[step, m, half] = jnp.dot(
                    ordered[...],
                    tiles[m, 2 * half + 1 - core].reshape(2 * PAIRS, QUART),
                    preferred_element_type=jnp.float32,
                )
            pair_copy(step, m).start()

        @pl.loop(0, 4)
        def _(i):
            m = lax.rem(level + 1 + i, 4)
            here = [
                jnp.dot(
                    ordered[...],
                    tiles[m, 2 * half + core].reshape(2 * PAIRS, QUART),
                    preferred_element_type=jnp.float32,
                )
                for half in range(2)
            ]
            pair_copy(step, m).wait_recv()
            for half in range(2):
                sent[step, 2 * m + half] = (here[half] + pair_got[step, m, half]).astype(jnp.bfloat16)
            for half in range(2):

                @pl.when(2 * m + half != a)
                def _():
                    partial_copy(step, 2 * m + half).start()

        got[step, a] = sent[step, a]
        partial_all(step).wait_recv()
        total = jnp.zeros((NX, QUART), jnp.float32)
        for source in range(ROWS):
            total += got[step, source].astype(jnp.float32)
        if step == 0:
            new = (levels * mine + total) / SPREAD
            state[0] = new
        elif step == 1:
            new = 2.0 * ((levels * state[0] + total) / SPREAD) - mine
            state[1] = new
        else:
            new = 2.0 * ((levels * state[1] + total) / SPREAD) - state[0]
        if step < 2:
            rounded[step] = swapped(new.astype(jnp.bfloat16))
            spread_start(step + 1, rounded.at[step])
        else:
            final_row[level] = new.astype(jnp.bfloat16)

    def row_copy(d):
        row = lax.rem(a + 2 * (d + 1), ROWS)
        return remote(final_row.at[level], final_row.at[level], sa.at[0], ra.at[0], row, b)

    for d in range(3):
        row_copy(d).start()

    for step in range(3):
        partial_all(step).wait_send()
        for m in range(4):
            pair_copy(step, m).wait_send()

        @pl.when(spread_own)
        def _():
            spread_all(step, 7).wait_send()

        @pl.when(jnp.logical_not(spread_own))
        def _():
            spread_all(step, 8).wait_send()

    remote(
        final_row.at[pl.ds(0, 3)], final_row.at[pl.ds(0, 3)], sa.at[0], ra.at[0], lax.rem(a + 1, ROWS), b
    ).wait()

    def last_copy(i):
        row, col = plane_device(i)
        return remote(final_sent.at[i], final_got.at[alpha], sb.at[0], rb.at[0], row, col)

    def last_local(label):
        return pltpu.make_async_copy(final_sent.at[4 * side + b // 4], final_got.at[label], rb.at[0])

    def last_self(i):
        return jnp.logical_and(plane_self, i == 4 * side + b // 4)

    for i in range(ROWS):
        final_sent[i] = final_row[value[8 * level + i] // 8]

        @pl.when(jnp.logical_not(last_self(i)))
        def _():
            last_copy(i).start()

        @pl.when(last_self(i))
        def _():
            last_local(alpha).start()

    def last_all(count):
        return remote(
            final_sent.at[pl.ds(0, count)],
            final_got.at[pl.ds(0, count)],
            sb.at[0],
            rb.at[0],
            lax.rem(a + 1, ROWS),
            b,
        )

    last_all(8).wait_recv()
    out_ref[...] = final_got[lax.rem(value[4 * a + b // 4], 8)].astype(jnp.float32)

    @pl.when(plane_self)
    def _():
        last_all(7).wait_send()

    @pl.when(jnp.logical_not(plane_self))
    def _():
        last_all(8).wait_send()


def per_device(orbitals, screened, kpoints, vectors, energies):
    dma = pltpu.SemaphoreType.DMA
    vmem = pl.BlockSpec(memory_space=pltpu.VMEM)
    smem = pl.BlockSpec(memory_space=pltpu.SMEM)
    anywhere = pl.BlockSpec(memory_space=pl.ANY)
    half, full = jnp.bfloat16, jnp.float32
    return pl.pallas_call(
        kernel,
        out_shape=jax.ShapeDtypeStruct((NX, QUART), full),
        in_specs=[smem, smem, vmem, anywhere, anywhere],
        out_specs=vmem,
        scratch_shapes=[
            pltpu.SMEM((NK,), jnp.int32),
            pltpu.VMEM((256, 128), full),
            pltpu.VMEM((4, 16, 128), half),
            pltpu.VMEM((NK, 16, 128), half),
            pltpu.VMEM((COLS, 6, 16, 128), half),
            pltpu.VMEM((COLS, 6, 16, 128), half),
            pltpu.VMEM((6, 64, NG), full),
            pltpu.VMEM((16, 128, NG), half),
            pltpu.VMEM((PAIRS, NG), half),
            pltpu.VMEM((PAIRS, NG), half),
            pltpu.VMEM((PAIRS, NG), half),
            pltpu.VMEM((2, 256, 256), full),
            pltpu.VMEM((4, 4, 2, PAIRS, QUART), half),
            pltpu.VMEM((QUART, QUART), half),
            pltpu.VMEM((4, NX, QUART), half),
            pltpu.VMEM((7, NX, QUART), half),
            pltpu.VMEM((8, NX, QUART), half),
            pltpu.VMEM((NX, QUART), half),
            pltpu.VMEM((NX, QUART), half),
            pltpu.VMEM((8, QUART), full),
            pltpu.VMEM((3, 8, NX, QUART), half),
            pltpu.VMEM((NX, 2 * PAIRS), half),
            pltpu.VMEM((3, ROWS, NX, QUART), half),
            pltpu.VMEM((3, ROWS, NX, QUART), half),
            pltpu.VMEM((3, 4, 2, NX, QUART), full),
            pltpu.VMEM((3, 4, 2, NX, QUART), full),
            pltpu.VMEM((2, NX, QUART), half),
            pltpu.VMEM((2, NX, QUART), full),
            pltpu.VMEM((4, NX, QUART), half),
            pltpu.VMEM((8, NX, QUART), half),
            pltpu.VMEM((8, NX, QUART), half),
            dma((1,)),
            dma((1,)),
            dma((1,)),
            dma((1,)),
            dma((8,)),
            dma((16,)),
            dma,
            dma((16,)),
            dma((1,)),
            dma((1,)),
            dma((3,)),
            dma((3,)),
            dma((3,)),
            dma((3,)),
            dma((3,)),
            dma((3,)),
            dma((1,)),
            dma((1,)),
            dma((1,)),
            dma((1,)),
            dma((3, 4)),
            dma((3, 4)),
        ],
        compiler_params=pltpu.CompilerParams(
            has_side_effects=True, collective_id=0, vmem_limit_bytes=56 << 20),
        name="mega",
    )(kpoints, energies, orbitals, screened, vectors)


def solution(mesh):
    placed = (P("row", "col", None), P(("row", "col"), None), P(), P(None, ("row", "col")), P())
    return jax.shard_map(
        per_device, mesh=mesh, in_specs=placed, out_specs=P(None, ("row", "col")), check_vma=False
    )
```

```python
import jax
import jax.numpy as jnp
from jax import lax
from jax.experimental import pallas as pl
from jax.experimental.pallas import tpu as pltpu
from jax.sharding import PartitionSpec as P

NV = 32
NC = 32
NG = 512
NX = 64
NK = 32
PAIRS = NV * NC
ROWS = 8
COLS = 16
SPREAD = 4.0
QUART = PAIRS // 4


def remote(src, dst, send_sem, recv_sem, row, col):
    return pltpu.make_async_remote_copy(
        src_ref=src,
        dst_ref=dst,
        send_sem=send_sem,
        recv_sem=recv_sem,
        device_id=(row, col),
        device_id_type=pl.DeviceIdType.MESH,
    )


def kernel(
    value,
    energy,
    orb_ref,
    screen_ref,
    vec_ref,
    out_ref,
    place,
    wide,
    orb_mine,
    orb_all,
    staged,
    landed,
    orb,
    screen,
    valence,
    conduct,
    amplitude,
    product,
    tiles,
    swap,
    vec_row,
    vec_sent,
    vec_got,
    own,
    own_swapped,
    gap,
    column,
    ordered,
    sent,
    got,
    pair_sent,
    pair_got,
    rounded,
    state,
    final_row,
    final_sent,
    final_got,
    s1,
    r1,
    s2,
    r2,
    sw,
    rw,
    lw,
    sf,
    sva,
    rva,
    svb,
    rvb,
    sg,
    rg,
    sp,
    rp,
    sa,
    ra,
    sb,
    rb,
    ss,
    rs,
):
    a = lax.axis_index("row")
    b = lax.axis_index("col")
    core = lax.rem(b, 2)
    alpha = b // 2
    level = a // 2
    side = lax.rem(a, 2)
    residue = 4 * side + b // 4
    piece = level * 4 + lax.rem(b, 4)
    needed = lax.rem(alpha - a + 8, 8)
    quarter = 2 * side + core
    point_value = alpha + 8 * level
    plane_self = lax.rem(alpha, 2) == side
    spread_core = lax.rem(level, 2)
    spread_own = jnp.logical_and(alpha == a, spread_core == core)

    def plane_device(i):
        return 2 * level + i // 4, 4 * lax.rem(i, 4) + quarter

    def plane_owner(label):
        return 2 * level + lax.rem(alpha, 2), 2 * label + core

    barrier = pltpu.get_barrier_semaphore()

    def greet(row, col):
        pl.semaphore_signal(barrier, inc=1, device_id=(row, col), device_id_type=pl.DeviceIdType.MESH)

    def greet_other(row, col):
        @pl.when(jnp.logical_or(row != a, col != b))
        def _():
            greet(row, col)

    @pl.loop(0, ROWS - 1)
    def _(d):
        greet(lax.rem(a + d + 1, ROWS), b)

    @pl.loop(0, COLS - 1)
    def _(d):
        greet(a, lax.rem(b + d + 1, COLS))

    @pl.loop(0, 8)
    def _(i):
        greet_other(2 * (i // 2) + needed // 4, 4 * lax.rem(needed, 4) + core + 2 * lax.rem(i, 2))
        greet_other(*plane_device(i))
        greet_other(*plane_owner(i))
        greet_other(4 * (i // 4) + 2 * core + lax.rem(i // 2, 2), 2 * a + lax.rem(i, 2))

    peers = ROWS - 1 + COLS - 1 + 32
    peers -= jnp.where(needed == residue, 1, 0)
    peers -= jnp.where(plane_self, 2, 0)
    peers -= jnp.where(spread_own, 1, 0)
    for k in range(4):
        for lanes in range(4):
            wide[pl.ds(k * 16 + lanes, 4, stride=4), :] = orb_ref[k, :, lanes * 128 : lanes * 128 + 128].astype(
                jnp.float32
            )
    for k in range(4):
        orb_mine[k] = wide[k * 16 : k * 16 + 16].astype(jnp.bfloat16)

    pl.semaphore_wait(barrier, peers)

    def first_copy(d):
        return remote(
            orb_mine, orb_all.at[pl.ds(4 * a, 4)], s1.at[0], r1.at[0], lax.rem(a + d + 1, ROWS), b
        )

    @pl.loop(0, ROWS - 1)
    def _(d):
        first_copy(d).start()

    orb_all[pl.ds(4 * a, 4)] = orb_mine[...]

    def vec_first_copy(label):
        row, col = plane_owner(label)
        slot = 4 * side + b // 4
        return remote(vec_ref, vec_got.at[slot], sva.at[0], rva.at[0], row, col)

    def vec_first_local():
        return pltpu.make_async_copy(vec_ref, vec_got.at[4 * side + b // 4], rva.at[0])

    def screen_target(label):
        return lax.rem(label - residue + 8, 8), 2 * label + core

    def screen_copy(i):
        row, col = screen_target(i)
        return remote(screen_ref, screen.at[piece], sw.at[i], rw.at[piece], row, col)

    def screen_local():
        return pltpu.make_async_copy(screen_ref, screen.at[piece], lw)

    def screen_self(i):
        row, col = screen_target(i)
        return jnp.logical_and(row == a, col == b)

    def forward_copy(p):
        return remote(screen.at[p], screen.at[p], sf.at[p], rw.at[p], a, b + 1 - 2 * core)

    def screen_start(i):
        label = lax.rem(i + alpha, 8)
        turn = lax.rem(level - screen_target(label)[0] // 2 + 4, 4) == i // 8

        @pl.when(jnp.logical_and(turn, screen_self(label)))
        def _():
            screen_local().start()

        @pl.when(jnp.logical_and(turn, jnp.logical_not(screen_self(label))))
        def _():
            screen_copy(label).start()


    @pl.loop(0, NK)
    def _(wanted):
        found = jnp.int32(0)
        for k in range(NK):
            found = jnp.where(value[k] == wanted, k, found)
        place[wanted] = found

    remote(orb_all.at[pl.ds(0, 28)], orb_all.at[pl.ds(0, 28)], s1.at[0], r1.at[0], lax.rem(a + 1, ROWS), b).wait()

    @pl.loop(0, COLS)
    def _(dest):
        for m in range(4):
            staged[dest, m] = orb_all[place[dest // 2 + 8 * m]]
        for t in range(2):
            staged[dest, 4 + t] = orb_all[place[a + 8 * lax.rem(dest, 2) + 16 * t]]

    def second_copy(d):
        col = lax.rem(b + d + 1, COLS)
        return remote(staged.at[col], landed.at[b], s2.at[0], r2.at[0], a, col)

    @pl.loop(0, COLS - 1)
    def _(d):
        second_copy(d).start()

    @pl.loop(0, 32)
    def _(i):
        screen_start(i)

    landed[b] = staged[b]

    def vec_start():
        @pl.loop(0, 8)
        def _(i):
            label = lax.rem(i + alpha, 8)
            here = jnp.logical_and(plane_self, label == alpha)

            @pl.when(here)
            def _():
                vec_first_local().start()

            @pl.when(jnp.logical_not(here))
            def _():
                vec_first_copy(label).start()

    def arrive(slot):
        for half in range(2):
            p = slot * 4 + core + 2 * half
            here = jnp.logical_and(needed == residue, p == piece)

            @pl.when(here)
            def _():
                screen_local().wait()

            @pl.when(jnp.logical_not(here))
            def _():
                remote(screen_ref, screen.at[p], sw.at[0], rw.at[p], lax.rem(a + 1, ROWS), b).wait_recv()

            forward_copy(p).start()

    def forwarded(slot):
        for half in range(2):
            p = slot * 4 + 1 - core + 2 * half
            forward_copy(p).wait_recv()

    row = lax.broadcasted_iota(jnp.int32, (QUART, QUART), 0)
    col = lax.broadcasted_iota(jnp.int32, (QUART, QUART), 1)
    hit = jnp.logical_and((row & 31) == (col >> 3), (row >> 5) == (col & 7))
    swap[...] = jnp.where(hit, 1.0, 0.0).astype(jnp.bfloat16)

    def swapped(block):
        return jnp.dot(block, swap[...], preferred_element_type=jnp.float32).astype(jnp.bfloat16)

    point = place[point_value]
    lane = lax.broadcasted_iota(jnp.int32, (8, QUART), 1)
    upper = jnp.zeros((8, QUART), jnp.float32)
    lower = jnp.zeros((8, QUART), jnp.float32)
    for c in range(NC):
        upper = jnp.where((lane & 31) == c, energy[point, NV + c], upper)
    for v in range(8):
        lower = jnp.where((lane >> 5) == v, energy[point, 8 * quarter + v], lower)
    gap[...] = upper - lower

    remote(
        staged.at[pl.ds(0, COLS - 1)], landed.at[pl.ds(0, COLS - 1)], s2.at[0], r2.at[0], a, lax.rem(b + 1, COLS)
    ).wait()

    @pl.loop(0, 6)
    def _(slot):
        for source in range(COLS):
            wide[source * 16 : source * 16 + 16] = landed[source, slot].astype(jnp.float32)
        for lanes in range(4):
            orb[slot, :, lanes * 128 : lanes * 128 + 128] = wide[pl.ds(lanes, 64, stride=4), :]

    def vec_second_copy(d):
        row = lax.rem(a + 2 * (d + 1), ROWS)
        return remote(vec_sent.at[d], vec_row.at[level], svb.at[d], rvb.at[d], row, b)

    part_index = (a // 4) * 4 + quarter

    def spread_copy(step, source, i):
        return remote(
            source,
            column.at[step, part_index],
            sg.at[step],
            rg.at[step],
            alpha,
            2 * lax.rem(alpha + i, 8) + spread_core,
        )

    def spread_local(step, source, p):
        return pltpu.make_async_copy(source, column.at[step, p], rg.at[step])

    def spread_self(i):
        return jnp.logical_and(i == 0, spread_own)

    def spread_start(step, source):
        @pl.loop(0, ROWS)
        def _(i):
            @pl.when(spread_self(i))
            def _():
                spread_local(step, source, part_index).start()

            @pl.when(jnp.logical_not(spread_self(i)))
            def _():
                spread_copy(step, source, i).start()

    def spread_all(step, count):
        return remote(
            column.at[step, pl.ds(0, count)],
            column.at[step, pl.ds(0, count)],
            sg.at[step],
            rg.at[step],
            lax.rem(a + 1, ROWS),
            b,
        )

    wrap = jnp.where(alpha >= a, 0, 1)
    lane = lax.broadcasted_iota(jnp.int32, (32, 128), 1)
    low = lane < 64
    even = (lane & 32) == 0

    def build(slot, m, t):
        left, right = m, 4 + t
        for v in range(NV):
            valence[v * 32 : v * 32 + 32] = (orb[left, v : v + 1] * orb[right, :NV]).astype(jnp.bfloat16)
            conduct[v * 32 : v * 32 + 32] = (orb[right, NV + v : NV + v + 1] * orb[left, NV:]).astype(
                jnp.bfloat16
            )
        block = screen[pl.ds(slot * 4, 4)].reshape(NG, NG)
        for chunk in range(4):
            rows = slice(chunk * 256, chunk * 256 + 256)
            amplitude[rows] = jnp.dot(valence[rows], block, preferred_element_type=jnp.float32).astype(
                jnp.bfloat16
            )

        def multiply(unit):
            block, chunk = divmod(unit, 4)
            product[unit % 2] = lax.dot_general(
                amplitude[chunk * 256 : chunk * 256 + 256],
                conduct[block * 256 : block * 256 + 256],
                (((1,), (1,)), ((), ())),
                preferred_element_type=jnp.float32,
            )

        def turn(unit):
            block, chunk = divmod(unit, 4)
            for octet in range(2):
                for half in range(2):
                    s = [
                        product[
                            unit % 2,
                            octet * 128 + i * 32 : octet * 128 + i * 32 + 32,
                            half * 128 : half * 128 + 128,
                        ]
                        for i in range(4)
                    ]
                    u0 = jnp.where(low, s[0], pltpu.roll(s[2], 64, 1))
                    u2 = jnp.where(low, pltpu.roll(s[0], 64, 1), s[2])
                    u1 = jnp.where(low, s[1], pltpu.roll(s[3], 64, 1))
                    u3 = jnp.where(low, pltpu.roll(s[1], 64, 1), s[3])
                    turned = [
                        jnp.where(even, u0, pltpu.roll(u1, 32, 1)),
                        jnp.where(even, pltpu.roll(u0, 96, 1), u1),
                        jnp.where(even, u2, pltpu.roll(u3, 32, 1)),
                        jnp.where(even, pltpu.roll(u2, 96, 1), u3),
                    ]
                    for j in range(4):
                        first = j * QUART + block * 64 + half * 32
                        tiles[m, chunk, t, first : first + 32, octet * 128 : octet * 128 + 128] = jnp.concatenate(
                            [turned[i][j * 8 : j * 8 + 8] for i in range(4)], axis=0
                        ).astype(jnp.bfloat16)

        multiply(0)
        for unit in range(1, 16):
            multiply(unit)
            turn(unit - 1)
        turn(15)

    arrive(level)

    @pl.loop(0, 4)
    def _(phase):
        slot = lax.rem(level + phase, 4)

        forwarded(slot)

        @pl.loop(0, 2)
        def _(t):
            @pl.when(jnp.logical_and(t == 1, phase < 3))
            def _():
                arrive(lax.rem(slot + 1, 4))

            build(slot, lax.rem(slot + wrap + core + 2 * t, 4), t)

        @pl.when(phase == 0)
        def _():
            vec_start()

        @pl.when(phase == 1)
        def _():
            def vec_all(count):
                return remote(
                    vec_got.at[pl.ds(0, count)],
                    vec_got.at[pl.ds(0, count)],
                    sva.at[0],
                    rva.at[0],
                    lax.rem(a + 1, ROWS),
                    b,
                )

            @pl.when(plane_self)
            def _():
                vec_all(7).wait_send()

            @pl.when(jnp.logical_not(plane_self))
            def _():
                vec_all(8).wait_send()

            vec_all(8).wait_recv()
            for d in range(3):
                home = alpha + 8 * lax.rem(level + d + 1, 4)
                vec_sent[d] = vec_got[lax.rem(place[home], 8)]
                vec_second_copy(d).start()
            vec_row[level] = vec_got[lax.rem(place[point_value], 8)]

        @pl.when(phase == 2)
        def _():
            for d in range(3):
                vec_second_copy(d).wait()
            own[...] = vec_row[place[point_value] // 8]
            own_swapped[...] = swapped(own[...])
            spread_start(0, own_swapped)

    @pl.loop(0, 8)
    def _(i):
        @pl.when(jnp.logical_not(screen_self(i)))
        def _():
            screen_copy(i).wait_send()

    for slot in range(4):
        for half in range(2):
            forward_copy(slot * 4 + core + 2 * half).wait_send()

    mine = own[...].astype(jnp.float32)
    levels = gap[0:1]

    def pair_copy(step, m):
        return remote(
            pair_sent.at[step, m],
            pair_got.at[step, m],
            ss.at[step, m],
            rs.at[step, m],
            a,
            b + 1 - 2 * core,
        )

    def partial_copy(step, row):
        return remote(sent.at[step, row], got.at[step, a], sp.at[step], rp.at[step], row, b)

    def partial_all(step):
        return remote(
            sent.at[step, pl.ds(0, ROWS - 1)],
            got.at[step, pl.ds(0, ROWS - 1)],
            sp.at[step],
            rp.at[step],
            lax.rem(a + 1, ROWS),
            b,
        )

    for step in range(3):
        spread_all(step, 8).wait_recv()
        for p in range(8):
            ordered[:, p * QUART : p * QUART + QUART] = column[step, p]

        for i in range(4):
            m = lax.rem(level + 1 + i, 4)
            for half in range(2):
                pair_sent[step, m, half] = jnp.dot(
                    ordered[...],
                    tiles[m, 2 * half + 1 - core].reshape(2 * PAIRS, QUART),
                    preferred_element_type=jnp.float32,
                )
            pair_copy(step, m).start()

        for i in range(4):
            m = lax.rem(level + 1 + i, 4)
            here = [
                jnp.dot(
                    ordered[...],
                    tiles[m, 2 * half + core].reshape(2 * PAIRS, QUART),
                    preferred_element_type=jnp.float32,
                )
                for half in range(2)
            ]
            pair_copy(step, m).wait_recv()
            for half in range(2):
                sent[step, 2 * m + half] = (here[half] + pair_got[step, m, half]).astype(jnp.bfloat16)
                if i < 3:
                    partial_copy(step, 2 * m + half).start()
        partial_copy(step, a + 1 - 2 * side).start()

        got[step, a] = sent[step, a]
        partial_all(step).wait_recv()
        total = jnp.zeros((NX, QUART), jnp.float32)
        for source in range(ROWS):
            total += got[step, source].astype(jnp.float32)
        if step == 0:
            new = (levels * mine + total) / SPREAD
            state[0] = new
        elif step == 1:
            new = 2.0 * ((levels * state[0] + total) / SPREAD) - mine
            state[1] = new
        else:
            new = 2.0 * ((levels * state[1] + total) / SPREAD) - state[0]
        if step < 2:
            rounded[step] = swapped(new.astype(jnp.bfloat16))
            spread_start(step + 1, rounded.at[step])
        else:
            final_row[level] = new.astype(jnp.bfloat16)

    def row_copy(d):
        row = lax.rem(a + 2 * (d + 1), ROWS)
        return remote(final_row.at[level], final_row.at[level], sa.at[0], ra.at[0], row, b)

    for d in range(3):
        row_copy(d).start()

    for step in range(3):
        partial_all(step).wait_send()
        for m in range(4):
            pair_copy(step, m).wait_send()

        @pl.when(spread_own)
        def _():
            spread_all(step, 7).wait_send()

        @pl.when(jnp.logical_not(spread_own))
        def _():
            spread_all(step, 8).wait_send()

    remote(
        final_row.at[pl.ds(0, 3)], final_row.at[pl.ds(0, 3)], sa.at[0], ra.at[0], lax.rem(a + 1, ROWS), b
    ).wait()

    def last_copy(i):
        row, col = plane_device(i)
        return remote(final_sent.at[i], final_got.at[alpha], sb.at[0], rb.at[0], row, col)

    def last_local(label):
        return pltpu.make_async_copy(final_sent.at[4 * side + b // 4], final_got.at[label], rb.at[0])

    def last_self(i):
        return jnp.logical_and(plane_self, i == 4 * side + b // 4)

    for i in range(ROWS):
        final_sent[i] = final_row[value[8 * level + i] // 8]

        @pl.when(jnp.logical_not(last_self(i)))
        def _():
            last_copy(i).start()

        @pl.when(last_self(i))
        def _():
            last_local(alpha).start()

    def last_all(count):
        return remote(
            final_sent.at[pl.ds(0, count)],
            final_got.at[pl.ds(0, count)],
            sb.at[0],
            rb.at[0],
            lax.rem(a + 1, ROWS),
            b,
        )

    last_all(8).wait_recv()
    out_ref[...] = final_got[lax.rem(value[4 * a + b // 4], 8)].astype(jnp.float32)

    @pl.when(plane_self)
    def _():
        last_all(7).wait_send()

    @pl.when(jnp.logical_not(plane_self))
    def _():
        last_all(8).wait_send()


def per_device(orbitals, screened, kpoints, vectors, energies):
    dma = pltpu.SemaphoreType.DMA
    vmem = pl.BlockSpec(memory_space=pltpu.VMEM)
    smem = pl.BlockSpec(memory_space=pltpu.SMEM)
    anywhere = pl.BlockSpec(memory_space=pl.ANY)
    half, full = jnp.bfloat16, jnp.float32
    return pl.pallas_call(
        kernel,
        out_shape=jax.ShapeDtypeStruct((NX, QUART), full),
        in_specs=[smem, smem, vmem, vmem, anywhere],
        out_specs=vmem,
        scratch_shapes=[
            pltpu.SMEM((NK,), jnp.int32),
            pltpu.VMEM((256, 128), full),
            pltpu.VMEM((4, 16, 128), half),
            pltpu.VMEM((NK, 16, 128), half),
            pltpu.VMEM((COLS, 6, 16, 128), half),
            pltpu.VMEM((COLS, 6, 16, 128), half),
            pltpu.VMEM((6, 64, NG), full),
            pltpu.VMEM((16, 128, NG), half),
            pltpu.VMEM((PAIRS, NG), half),
            pltpu.VMEM((PAIRS, NG), half),
            pltpu.VMEM((PAIRS, NG), half),
            pltpu.VMEM((2, 256, 256), full),
            pltpu.VMEM((4, 4, 2, PAIRS, QUART), half),
            pltpu.VMEM((QUART, QUART), half),
            pltpu.VMEM((4, NX, QUART), half),
            pltpu.VMEM((7, NX, QUART), half),
            pltpu.VMEM((8, NX, QUART), half),
            pltpu.VMEM((NX, QUART), half),
            pltpu.VMEM((NX, QUART), half),
            pltpu.VMEM((8, QUART), full),
            pltpu.VMEM((3, 8, NX, QUART), half),
            pltpu.VMEM((NX, 2 * PAIRS), half),
            pltpu.VMEM((3, ROWS, NX, QUART), half),
            pltpu.VMEM((3, ROWS, NX, QUART), half),
            pltpu.VMEM((3, 4, 2, NX, QUART), full),
            pltpu.VMEM((3, 4, 2, NX, QUART), full),
            pltpu.VMEM((2, NX, QUART), half),
            pltpu.VMEM((2, NX, QUART), full),
            pltpu.VMEM((4, NX, QUART), half),
            pltpu.VMEM((8, NX, QUART), half),
            pltpu.VMEM((8, NX, QUART), half),
            dma((1,)),
            dma((1,)),
            dma((1,)),
            dma((1,)),
            dma((8,)),
            dma((16,)),
            dma,
            dma((16,)),
            dma((1,)),
            dma((1,)),
            dma((3,)),
            dma((3,)),
            dma((3,)),
            dma((3,)),
            dma((3,)),
            dma((3,)),
            dma((1,)),
            dma((1,)),
            dma((1,)),
            dma((1,)),
            dma((3, 4)),
            dma((3, 4)),
        ],
        compiler_params=pltpu.CompilerParams(
            has_side_effects=True, collective_id=0, vmem_limit_bytes=56 << 20),
        name="mega",
    )(kpoints, energies, orbitals, screened, vectors)


def solution(mesh):
    placed = (P("row", "col", None), P(("row", "col"), None), P(), P(None, ("row", "col")), P())
    return jax.shard_map(
        per_device, mesh=mesh, in_specs=placed, out_specs=P(None, ("row", "col")), check_vma=False
    )
```

```python
import jax
import jax.numpy as jnp
from jax import lax
from jax.experimental import pallas as pl
from jax.experimental.pallas import tpu as pltpu
from jax.sharding import PartitionSpec as P

NV = 32
NC = 32
NG = 512
NX = 64
NK = 32
PAIRS = NV * NC
ROWS = 8
COLS = 16
SPREAD = 4.0
QUART = PAIRS // 4


def remote(src, dst, send_sem, recv_sem, row, col):
    return pltpu.make_async_remote_copy(
        src_ref=src,
        dst_ref=dst,
        send_sem=send_sem,
        recv_sem=recv_sem,
        device_id=(row, col),
        device_id_type=pl.DeviceIdType.MESH,
    )


def kernel(
    value,
    energy,
    orb_ref,
    screen_ref,
    vec_ref,
    out_ref,
    place,
    wide,
    orb_mine,
    orb_all,
    staged,
    landed,
    orb,
    screen,
    valence,
    conduct,
    amplitude,
    product,
    tiles,
    swap,
    vec_row,
    vec_sent,
    vec_got,
    own,
    own_swapped,
    gap,
    column,
    ordered,
    sent,
    got,
    pair_sent,
    pair_got,
    rounded,
    state,
    final_row,
    final_sent,
    final_got,
    s1,
    r1,
    s2,
    r2,
    sw,
    rw,
    lw,
    sf,
    sva,
    rva,
    svb,
    rvb,
    sg,
    rg,
    sp,
    rp,
    sa,
    ra,
    sb,
    rb,
    ss,
    rs,
):
    a = lax.axis_index("row")
    b = lax.axis_index("col")
    core = lax.rem(b, 2)
    alpha = b // 2
    level = a // 2
    side = lax.rem(a, 2)
    residue = 4 * side + b // 4
    piece = level * 4 + lax.rem(b, 4)
    needed = lax.rem(alpha - a + 8, 8)
    quarter = 2 * side + core
    point_value = alpha + 8 * level
    plane_self = lax.rem(alpha, 2) == side
    spread_core = lax.rem(level, 2)
    spread_own = jnp.logical_and(alpha == a, spread_core == core)

    def plane_device(i):
        return 2 * level + i // 4, 4 * lax.rem(i, 4) + quarter

    def plane_owner(label):
        return 2 * level + lax.rem(alpha, 2), 2 * label + core

    barrier = pltpu.get_barrier_semaphore()

    def greet(row, col):
        pl.semaphore_signal(barrier, inc=1, device_id=(row, col), device_id_type=pl.DeviceIdType.MESH)

    def greet_other(row, col):
        @pl.when(jnp.logical_or(row != a, col != b))
        def _():
            greet(row, col)

    @pl.loop(0, ROWS - 1)
    def _(d):
        greet(lax.rem(a + d + 1, ROWS), b)

    @pl.loop(0, COLS - 1)
    def _(d):
        greet(a, lax.rem(b + d + 1, COLS))

    @pl.loop(0, 8)
    def _(i):
        greet_other(2 * (i // 2) + needed // 4, 4 * lax.rem(needed, 4) + core + 2 * lax.rem(i, 2))
        greet_other(*plane_device(i))
        greet_other(*plane_owner(i))
        greet_other(4 * (i // 4) + 2 * core + lax.rem(i // 2, 2), 2 * a + lax.rem(i, 2))

    peers = ROWS - 1 + COLS - 1 + 32
    peers -= jnp.where(needed == residue, 1, 0)
    peers -= jnp.where(plane_self, 2, 0)
    peers -= jnp.where(spread_own, 1, 0)
    for k in range(4):
        for lanes in range(4):
            wide[pl.ds(k * 16 + lanes, 4, stride=4), :] = orb_ref[k, :, lanes * 128 : lanes * 128 + 128].astype(
                jnp.float32
            )
    for k in range(4):
        orb_mine[k] = wide[k * 16 : k * 16 + 16].astype(jnp.bfloat16)

    pl.semaphore_wait(barrier, peers)

    def first_copy(d):
        return remote(
            orb_mine, orb_all.at[pl.ds(4 * a, 4)], s1.at[0], r1.at[0], lax.rem(a + d + 1, ROWS), b
        )

    @pl.loop(0, ROWS - 1)
    def _(d):
        first_copy(d).start()

    orb_all[pl.ds(4 * a, 4)] = orb_mine[...]

    def vec_first_copy(label):
        row, col = plane_owner(label)
        slot = 4 * side + b // 4
        return remote(vec_ref, vec_got.at[slot], sva.at[0], rva.at[0], row, col)

    def vec_first_local():
        return pltpu.make_async_copy(vec_ref, vec_got.at[4 * side + b // 4], rva.at[0])

    def screen_target(label):
        return lax.rem(label - residue + 8, 8), 2 * label + core

    def screen_copy(i):
        row, col = screen_target(i)
        return remote(screen_ref, screen.at[piece], sw.at[i], rw.at[piece], row, col)

    def screen_local():
        return pltpu.make_async_copy(screen_ref, screen.at[piece], lw)

    def screen_self(i):
        row, col = screen_target(i)
        return jnp.logical_and(row == a, col == b)

    def forward_copy(p):
        return remote(screen.at[p], screen.at[p], sf.at[p], rw.at[p], a, b + 1 - 2 * core)

    def screen_start(i):
        label = lax.rem(i + alpha, 8)
        turn = lax.rem(level - screen_target(label)[0] // 2 + 4, 4) == i // 8

        @pl.when(jnp.logical_and(turn, screen_self(label)))
        def _():
            screen_local().start()

        @pl.when(jnp.logical_and(turn, jnp.logical_not(screen_self(label))))
        def _():
            screen_copy(label).start()


    @pl.loop(0, NK)
    def _(wanted):
        found = jnp.int32(0)
        for k in range(NK):
            found = jnp.where(value[k] == wanted, k, found)
        place[wanted] = found

    remote(orb_all.at[pl.ds(0, 28)], orb_all.at[pl.ds(0, 28)], s1.at[0], r1.at[0], lax.rem(a + 1, ROWS), b).wait()

    @pl.loop(0, COLS)
    def _(dest):
        for m in range(4):
            staged[dest, m] = orb_all[place[dest // 2 + 8 * m]]
        for t in range(2):
            staged[dest, 4 + t] = orb_all[place[a + 8 * lax.rem(dest, 2) + 16 * t]]

    def second_copy(d):
        col = lax.rem(b + d + 1, COLS)
        return remote(staged.at[col], landed.at[b], s2.at[0], r2.at[0], a, col)

    @pl.loop(0, COLS - 1)
    def _(d):
        second_copy(d).start()

    @pl.loop(0, 32)
    def _(i):
        screen_start(i)

    landed[b] = staged[b]

    def vec_start():
        @pl.loop(0, 8)
        def _(i):
            label = lax.rem(i + alpha, 8)
            here = jnp.logical_and(plane_self, label == alpha)

            @pl.when(here)
            def _():
                vec_first_local().start()

            @pl.when(jnp.logical_not(here))
            def _():
                vec_first_copy(label).start()

    def arrive(slot):
        for half in range(2):
            p = slot * 4 + core + 2 * half
            here = jnp.logical_and(needed == residue, p == piece)

            @pl.when(here)
            def _():
                screen_local().wait()

            @pl.when(jnp.logical_not(here))
            def _():
                remote(screen_ref, screen.at[p], sw.at[0], rw.at[p], lax.rem(a + 1, ROWS), b).wait_recv()

            forward_copy(p).start()

    def forwarded(slot):
        for half in range(2):
            p = slot * 4 + 1 - core + 2 * half
            forward_copy(p).wait_recv()

    row = lax.broadcasted_iota(jnp.int32, (QUART, QUART), 0)
    col = lax.broadcasted_iota(jnp.int32, (QUART, QUART), 1)
    hit = jnp.logical_and((row & 31) == (col >> 3), (row >> 5) == (col & 7))
    swap[...] = jnp.where(hit, 1.0, 0.0).astype(jnp.bfloat16)

    def swapped(block):
        return jnp.dot(block, swap[...], preferred_element_type=jnp.float32).astype(jnp.bfloat16)

    point = place[point_value]
    lane = lax.broadcasted_iota(jnp.int32, (8, QUART), 1)
    upper = jnp.zeros((8, QUART), jnp.float32)
    lower = jnp.zeros((8, QUART), jnp.float32)
    for c in range(NC):
        upper = jnp.where((lane & 31) == c, energy[point, NV + c], upper)
    for v in range(8):
        lower = jnp.where((lane >> 5) == v, energy[point, 8 * quarter + v], lower)
    gap[...] = upper - lower

    remote(
        staged.at[pl.ds(0, COLS - 1)], landed.at[pl.ds(0, COLS - 1)], s2.at[0], r2.at[0], a, lax.rem(b + 1, COLS)
    ).wait()

    @pl.loop(0, 6)
    def _(slot):
        for source in range(COLS):
            wide[source * 16 : source * 16 + 16] = landed[source, slot].astype(jnp.float32)
        for lanes in range(4):
            orb[slot, :, lanes * 128 : lanes * 128 + 128] = wide[pl.ds(lanes, 64, stride=4), :]

    def vec_second_copy(d):
        row = lax.rem(a + 2 * (d + 1), ROWS)
        return remote(vec_sent.at[d], vec_row.at[level], svb.at[d], rvb.at[d], row, b)

    part_index = (a // 4) * 4 + quarter

    def spread_copy(step, source, i):
        return remote(
            source,
            column.at[step, part_index],
            sg.at[step],
            rg.at[step],
            alpha,
            2 * lax.rem(alpha + i, 8) + spread_core,
        )

    def spread_local(step, source, p):
        return pltpu.make_async_copy(source, column.at[step, p], rg.at[step])

    def spread_self(i):
        return jnp.logical_and(i == 0, spread_own)

    def spread_start(step, source):
        @pl.loop(0, ROWS)
        def _(i):
            @pl.when(spread_self(i))
            def _():
                spread_local(step, source, part_index).start()

            @pl.when(jnp.logical_not(spread_self(i)))
            def _():
                spread_copy(step, source, i).start()

    def spread_all(step, count):
        return remote(
            column.at[step, pl.ds(0, count)],
            column.at[step, pl.ds(0, count)],
            sg.at[step],
            rg.at[step],
            lax.rem(a + 1, ROWS),
            b,
        )

    wrap = jnp.where(alpha >= a, 0, 1)
    lane = lax.broadcasted_iota(jnp.int32, (32, 128), 1)
    low = lane < 64
    even = (lane & 32) == 0

    def build(slot, m, t):
        left, right = m, 4 + t
        for v in range(NV):
            valence[v * 32 : v * 32 + 32] = (orb[left, v : v + 1] * orb[right, :NV]).astype(jnp.bfloat16)
            conduct[v * 32 : v * 32 + 32] = (orb[right, NV + v : NV + v + 1] * orb[left, NV:]).astype(
                jnp.bfloat16
            )
        block = screen[pl.ds(slot * 4, 4)].reshape(NG, NG)
        for chunk in range(4):
            rows = slice(chunk * 256, chunk * 256 + 256)
            amplitude[rows] = jnp.dot(valence[rows], block, preferred_element_type=jnp.float32).astype(
                jnp.bfloat16
            )

        def multiply(unit):
            block, chunk = divmod(unit, 4)
            product[unit % 2] = lax.dot_general(
                amplitude[chunk * 256 : chunk * 256 + 256],
                conduct[block * 256 : block * 256 + 256],
                (((1,), (1,)), ((), ())),
                preferred_element_type=jnp.float32,
            )

        def turn(unit):
            block, chunk = divmod(unit, 4)
            for octet in range(2):
                for half in range(2):
                    s = [
                        product[
                            unit % 2,
                            octet * 128 + i * 32 : octet * 128 + i * 32 + 32,
                            half * 128 : half * 128 + 128,
                        ]
                        for i in range(4)
                    ]
                    u0 = jnp.where(low, s[0], pltpu.roll(s[2], 64, 1))
                    u2 = jnp.where(low, pltpu.roll(s[0], 64, 1), s[2])
                    u1 = jnp.where(low, s[1], pltpu.roll(s[3], 64, 1))
                    u3 = jnp.where(low, pltpu.roll(s[1], 64, 1), s[3])
                    turned = [
                        jnp.where(even, u0, pltpu.roll(u1, 32, 1)),
                        jnp.where(even, pltpu.roll(u0, 96, 1), u1),
                        jnp.where(even, u2, pltpu.roll(u3, 32, 1)),
                        jnp.where(even, pltpu.roll(u2, 96, 1), u3),
                    ]
                    for j in range(4):
                        first = j * QUART + block * 64 + half * 32
                        tiles[m, chunk, t, first : first + 32, octet * 128 : octet * 128 + 128] = jnp.concatenate(
                            [turned[i][j * 8 : j * 8 + 8] for i in range(4)], axis=0
                        ).astype(jnp.bfloat16)

        multiply(0)
        for unit in range(1, 16):
            multiply(unit)
            turn(unit - 1)
        turn(15)

    arrive(level)

    @pl.loop(0, 4)
    def _(phase):
        slot = lax.rem(level + phase, 4)

        forwarded(slot)

        @pl.loop(0, 2)
        def _(t):
            @pl.when(jnp.logical_and(t == 1, phase < 3))
            def _():
                arrive(lax.rem(slot + 1, 4))

            build(slot, lax.rem(slot + wrap + core + 2 * t, 4), t)

        @pl.when(phase == 0)
        def _():
            vec_start()

        @pl.when(phase == 1)
        def _():
            def vec_all(count):
                return remote(
                    vec_got.at[pl.ds(0, count)],
                    vec_got.at[pl.ds(0, count)],
                    sva.at[0],
                    rva.at[0],
                    lax.rem(a + 1, ROWS),
                    b,
                )

            @pl.when(plane_self)
            def _():
                vec_all(7).wait_send()

            @pl.when(jnp.logical_not(plane_self))
            def _():
                vec_all(8).wait_send()

            vec_all(8).wait_recv()
            for d in range(3):
                home = alpha + 8 * lax.rem(level + d + 1, 4)
                vec_sent[d] = vec_got[lax.rem(place[home], 8)]
                vec_second_copy(d).start()
            vec_row[level] = vec_got[lax.rem(place[point_value], 8)]

        @pl.when(phase == 2)
        def _():
            for d in range(3):
                vec_second_copy(d).wait()
            own[...] = vec_row[place[point_value] // 8]
            own_swapped[...] = swapped(own[...])
            spread_start(0, own_swapped)

    @pl.loop(0, 8)
    def _(i):
        @pl.when(jnp.logical_not(screen_self(i)))
        def _():
            screen_copy(i).wait_send()

    for slot in range(4):
        for half in range(2):
            forward_copy(slot * 4 + core + 2 * half).wait_send()

    mine = own[...].astype(jnp.float32)
    levels = gap[0:1]

    def pair_copy(step, m):
        return remote(
            pair_sent.at[step, m],
            pair_got.at[step, m],
            ss.at[step, m],
            rs.at[step, m],
            a,
            b + 1 - 2 * core,
        )

    def partial_copy(step, row):
        return remote(sent.at[step, row], got.at[step, a], sp.at[step], rp.at[step], row, b)

    def partial_all(step):
        return remote(
            sent.at[step, pl.ds(0, ROWS - 1)],
            got.at[step, pl.ds(0, ROWS - 1)],
            sp.at[step],
            rp.at[step],
            lax.rem(a + 1, ROWS),
            b,
        )

    for step in range(3):
        spread_all(step, 8).wait_recv()
        for p in range(8):
            ordered[:, p * QUART : p * QUART + QUART] = column[step, p]

        for i in range(4):
            m = lax.rem(level + (2, 1, 3, 0)[i], 4)
            for half in range(2):
                pair_sent[step, m, half] = jnp.dot(
                    ordered[...],
                    tiles[m, 2 * half + 1 - core].reshape(2 * PAIRS, QUART),
                    preferred_element_type=jnp.float32,
                )
            pair_copy(step, m).start()

        for i in range(4):
            m = lax.rem(level + (2, 1, 3, 0)[i], 4)
            here = [
                jnp.dot(
                    ordered[...],
                    tiles[m, 2 * half + core].reshape(2 * PAIRS, QUART),
                    preferred_element_type=jnp.float32,
                )
                for half in range(2)
            ]
            pair_copy(step, m).wait_recv()
            for half in range(2):
                sent[step, 2 * m + half] = (here[half] + pair_got[step, m, half]).astype(jnp.bfloat16)
                if i < 3:
                    partial_copy(step, 2 * m + half).start()
        partial_copy(step, a + 1 - 2 * side).start()

        got[step, a] = sent[step, a]
        partial_all(step).wait_recv()
        total = jnp.zeros((NX, QUART), jnp.float32)
        for source in range(ROWS):
            total += got[step, source].astype(jnp.float32)
        if step == 0:
            new = (levels * mine + total) / SPREAD
            state[0] = new
        elif step == 1:
            new = 2.0 * ((levels * state[0] + total) / SPREAD) - mine
            state[1] = new
        else:
            new = 2.0 * ((levels * state[1] + total) / SPREAD) - state[0]
        if step < 2:
            rounded[step] = swapped(new.astype(jnp.bfloat16))
            spread_start(step + 1, rounded.at[step])
        else:
            final_row[level] = new.astype(jnp.bfloat16)

    def row_copy(d):
        row = lax.rem(a + 2 * (d + 1), ROWS)
        return remote(final_row.at[level], final_row.at[level], sa.at[0], ra.at[0], row, b)

    for d in range(3):
        row_copy(d).start()

    for step in range(3):
        partial_all(step).wait_send()
        for m in range(4):
            pair_copy(step, m).wait_send()

        @pl.when(spread_own)
        def _():
            spread_all(step, 7).wait_send()

        @pl.when(jnp.logical_not(spread_own))
        def _():
            spread_all(step, 8).wait_send()

    remote(
        final_row.at[pl.ds(0, 3)], final_row.at[pl.ds(0, 3)], sa.at[0], ra.at[0], lax.rem(a + 1, ROWS), b
    ).wait()

    def last_copy(i):
        row, col = plane_device(i)
        return remote(final_sent.at[i], final_got.at[alpha], sb.at[0], rb.at[0], row, col)

    def last_local(label):
        return pltpu.make_async_copy(final_sent.at[4 * side + b // 4], final_got.at[label], rb.at[0])

    def last_self(i):
        return jnp.logical_and(plane_self, i == 4 * side + b // 4)

    for i in range(ROWS):
        final_sent[i] = final_row[value[8 * level + i] // 8]

        @pl.when(jnp.logical_not(last_self(i)))
        def _():
            last_copy(i).start()

        @pl.when(last_self(i))
        def _():
            last_local(alpha).start()

    def last_all(count):
        return remote(
            final_sent.at[pl.ds(0, count)],
            final_got.at[pl.ds(0, count)],
            sb.at[0],
            rb.at[0],
            lax.rem(a + 1, ROWS),
            b,
        )

    last_all(8).wait_recv()
    out_ref[...] = final_got[lax.rem(value[4 * a + b // 4], 8)].astype(jnp.float32)

    @pl.when(plane_self)
    def _():
        last_all(7).wait_send()

    @pl.when(jnp.logical_not(plane_self))
    def _():
        last_all(8).wait_send()


def per_device(orbitals, screened, kpoints, vectors, energies):
    dma = pltpu.SemaphoreType.DMA
    vmem = pl.BlockSpec(memory_space=pltpu.VMEM)
    smem = pl.BlockSpec(memory_space=pltpu.SMEM)
    anywhere = pl.BlockSpec(memory_space=pl.ANY)
    half, full = jnp.bfloat16, jnp.float32
    return pl.pallas_call(
        kernel,
        out_shape=jax.ShapeDtypeStruct((NX, QUART), full),
        in_specs=[smem, smem, vmem, vmem, anywhere],
        out_specs=vmem,
        scratch_shapes=[
            pltpu.SMEM((NK,), jnp.int32),
            pltpu.VMEM((256, 128), full),
            pltpu.VMEM((4, 16, 128), half),
            pltpu.VMEM((NK, 16, 128), half),
            pltpu.VMEM((COLS, 6, 16, 128), half),
            pltpu.VMEM((COLS, 6, 16, 128), half),
            pltpu.VMEM((6, 64, NG), full),
            pltpu.VMEM((16, 128, NG), half),
            pltpu.VMEM((PAIRS, NG), half),
            pltpu.VMEM((PAIRS, NG), half),
            pltpu.VMEM((PAIRS, NG), half),
            pltpu.VMEM((2, 256, 256), full),
            pltpu.VMEM((4, 4, 2, PAIRS, QUART), half),
            pltpu.VMEM((QUART, QUART), half),
            pltpu.VMEM((4, NX, QUART), half),
            pltpu.VMEM((7, NX, QUART), half),
            pltpu.VMEM((8, NX, QUART), half),
            pltpu.VMEM((NX, QUART), half),
            pltpu.VMEM((NX, QUART), half),
            pltpu.VMEM((8, QUART), full),
            pltpu.VMEM((3, 8, NX, QUART), half),
            pltpu.VMEM((NX, 2 * PAIRS), half),
            pltpu.VMEM((3, ROWS, NX, QUART), half),
            pltpu.VMEM((3, ROWS, NX, QUART), half),
            pltpu.VMEM((3, 4, 2, NX, QUART), full),
            pltpu.VMEM((3, 4, 2, NX, QUART), full),
            pltpu.VMEM((2, NX, QUART), half),
            pltpu.VMEM((2, NX, QUART), full),
            pltpu.VMEM((4, NX, QUART), half),
            pltpu.VMEM((8, NX, QUART), half),
            pltpu.VMEM((8, NX, QUART), half),
            dma((1,)),
            dma((1,)),
            dma((1,)),
            dma((1,)),
            dma((8,)),
            dma((16,)),
            dma,
            dma((16,)),
            dma((1,)),
            dma((1,)),
            dma((3,)),
            dma((3,)),
            dma((3,)),
            dma((3,)),
            dma((3,)),
            dma((3,)),
            dma((1,)),
            dma((1,)),
            dma((1,)),
            dma((1,)),
            dma((3, 4)),
            dma((3, 4)),
        ],
        compiler_params=pltpu.CompilerParams(
            has_side_effects=True, collective_id=0, vmem_limit_bytes=56 << 20),
        name="mega",
    )(kpoints, energies, orbitals, screened, vectors)


def solution(mesh):
    placed = (P("row", "col", None), P(("row", "col"), None), P(), P(None, ("row", "col")), P())
    return jax.shard_map(
        per_device, mesh=mesh, in_specs=placed, out_specs=P(None, ("row", "col")), check_vma=False
    )
```
